512 devices in a mesh: dp: 16 (over y, x_lo, core), vocab: 32 (over x_hi, z).
Axes of the slice: x: 4 (x_hi: 2, x_lo: 2; x = x_hi * 2 + x_lo), y: 4, z: 16, core: 2. Of those that a mesh axis runs over, the one named last changes fastest.
Arguments:
- hidden_states: bfloat16 [4, 4096, 8192], P(None, 'dp', 'vocab'), may hold values from -400 to 400
- exit_layers: int32 [64, 2], P('dp'), may hold values from 0 to 3, all different within a row
- targets: int32 [4096], P('dp'), may hold values from 0 to 8191
- norm_gain: bfloat16 [8192], replicated, may hold values from 0.25 to 1.75
- exit_scale: float32 [2], replicated, may hold values from 0.5 to 2
- unembedding: bfloat16 [8192, 8192], P(None, 'vocab'), may hold values from -3 to 3
Outputs:
- weight_grad: float32 [8192, 8192], P('dp', 'vocab')
- mean_loss: float32 [], replicated
The draws below stay inside these ranges and needn't reach their ends.
Inputs may be any that keep to these rules, and one draw needn't show every extreme that they name: `exit_layers`: each row of 64 tokens names 2 different layers, and every layer is named by some row.
All inputs are finite; a program needn't handle non-finite values.
Results may differ from the reference program's by a relative error of at most 0.013.
Values may be sent and summed in bfloat16 or wider, within the bound.
A program may use at most 128 MiB of HBM per device.

```python
import math
import jax
import jax.numpy as jnp
from jax import lax

D = 8192
VOCAB_DEV = 256
LAYERS = 4
EXITS = 2
SEQ = 64
TOK_DEV = 256
TOKENS = 4096
ROWS = 64
VOCAB = 8192
N_DP = 16


def pair_columns(key):
    first_cols = jax.random.permutation(jax.random.fold_in(key, 103), VOCAB)[:8]
    return (first_cols, (first_cols + VOCAB_DEV) % VOCAB)


def align_size():
    return min(max(3.0 / math.sqrt(D), 190.0 / D), 2.95)


def sign_columns(key):
    flips = jax.random.randint(jax.random.fold_in(key, 104), (8, D), 0, 2).astype(jnp.float32)
    return 2.0 * flips - 1.0


def make_unembed(key):
    base_field = jnp.clip(jax.random.normal(jax.random.fold_in(key, 101), (D, VOCAB), jnp.float32), -6.0, 6.0)
    weights = base_field * (3.0 / math.sqrt(D))
    first_cols, second_cols = pair_columns(key)
    special = sign_columns(key).T * align_size()
    weights = weights.at[:, first_cols].set(special)
    weights = weights.at[:, second_cols].set(0.98 * special + 0.1 * weights[:, second_cols])
    return jnp.clip(weights, -3.0, 3.0)


def draw_unembedding(key, part):
    return make_unembed(key).astype(jnp.bfloat16)


def draw_hidden_states(key, part):
    base_field = jnp.clip(jax.random.normal(jax.random.fold_in(key, 111), (LAYERS, TOKENS, D), jnp.float32), -5.0, 5.0)
    col_scale = 1.0 + 2.0 * jnp.arange(D, dtype=jnp.float32) / D
    row_scale = jnp.exp(jax.random.uniform(jax.random.fold_in(key, 113), (LAYERS, TOKENS, 1), jnp.float32, 0.0, math.log(10.0)))
    field = base_field * col_scale
    weights = make_unembed(key)
    positions = jnp.arange(TOKENS, dtype=jnp.int32)
    place = positions.astype(jnp.float32) / TOKENS
    lift = 0.95 * place
    token_cols = jax.random.randint(jax.random.fold_in(key, 116), (TOKENS,), 0, VOCAB)
    toward = weights.T[token_cols] * (math.sqrt(D) / 3.0)
    field = jnp.sqrt(1.0 - lift * lift)[None, :, None] * field + lift[None, :, None] * toward[None]
    is_aligned = positions % 37 == 3
    pair_slot = positions % 8
    strength = 0.7 + 0.15 * (positions // 37 % 3).astype(jnp.float32)
    aligned = sign_columns(key)[pair_slot]
    mixed = strength[:, None] * aligned + jnp.sqrt(1.0 - strength * strength)[:, None] * base_field
    field = jnp.where(is_aligned[None, :, None], mixed, field)
    return jnp.clip(field * row_scale, -400.0, 400.0).astype(jnp.bfloat16)


def set_ends(array, own_key, low, high):
    spot = [jax.random.randint(jax.random.fold_in(own_key, axis), (), 0, length) for axis, length in enumerate(array.shape)]
    main_axis = array.shape.index(max(array.shape))
    next_to = spot[:main_axis] + [(spot[main_axis] + 1) % array.shape[main_axis]] + spot[main_axis + 1:]
    return array.at[tuple(spot)].set(low).at[tuple(next_to)].set(high)


def choose_distinct(stream_key, rows, number_of, top, lift):
    sequence = jax.random.permutation(jax.random.fold_in(stream_key, 1), number_of)
    boost = sequence
    for power in range(3):
        boost = boost * boost // number_of
    boost = boost * lift // number_of
    lots = jax.random.randint(jax.random.fold_in(stream_key, 2), (rows, number_of), 0, 4096) + boost
    fixed_rows = jax.random.permutation(jax.random.fold_in(stream_key, 3), rows)[jnp.arange(number_of) % rows]
    lots = jnp.where(jnp.arange(rows)[:, None] == fixed_rows[None, :], 1 << 14, lots)
    score = lots * number_of + jnp.arange(number_of)
    return lax.top_k(score.astype(jnp.int32), top)[1].astype(jnp.int32)


def setup_inputs(seed: int = 0) -> dict:
    key_of = jax.random.split(jax.random.key(seed), 7)
    hidden_states = draw_hidden_states(jax.random.fold_in(key_of[6], 71), 0)
    exit_layers = choose_distinct(key_of[1], ROWS, LAYERS, EXITS, 0)
    targets = set_ends(jax.random.randint(key_of[2], (TOKENS,), 0, VOCAB), jax.random.fold_in(key_of[2], 1), 0, VOCAB - 1).astype(jnp.int32)
    norm_gain = jnp.clip(1.0 + 0.15 * jax.random.normal(key_of[3], (D,), jnp.float32), 0.25, 1.75).astype(jnp.bfloat16)
    exit_scale = jnp.clip(jnp.exp(jax.random.uniform(key_of[4], (EXITS,), jnp.float32, math.log(0.5), math.log(2.0))), 0.5, 2.0)
    unembedding = draw_unembedding(jax.random.fold_in(key_of[6], 71), 0)
    return {"hidden_states": hidden_states, "exit_layers": exit_layers, "targets": targets, "norm_gain": norm_gain, "exit_scale": exit_scale, "unembedding": unembedding}


norm_eps = 1e-05

def reference(hidden_states, exit_layers, targets, norm_gain, exit_scale, unembedding):
    positions = jnp.arange(TOKENS, dtype=jnp.int32)
    row_layers = jnp.repeat(exit_layers, SEQ, axis=0)
    selected = jnp.stack([hidden_states[row_layers[:, index], positions] for index in range(EXITS)])
    values = selected.astype(jnp.float32)
    mean_sq = lax.optimization_barrier(jnp.mean(values * values, axis=-1, keepdims=True))
    normed = (values * lax.rsqrt(mean_sq + norm_eps) * norm_gain.astype(jnp.float32)).astype(jnp.bfloat16)
    grouped = normed.reshape(EXITS, N_DP, TOK_DEV, D).transpose(1, 0, 2, 3).reshape(N_DP, EXITS * TOK_DEV, D)
    group_targets = jnp.tile(targets.reshape(N_DP, TOK_DEV), (1, EXITS))
    scale_rows = jnp.repeat(exit_scale, TOK_DEV)
    columns = jnp.arange(VOCAB, dtype=jnp.int32)

    def one_group(state_pair, inputs):
        grad_total, loss_total = state_pair
        group_rows, labels = inputs
        logits = jnp.dot(group_rows, unembedding, preferred_element_type=jnp.float32)
        row_top = lax.optimization_barrier(jnp.max(logits, axis=-1))
        log_total = row_top + jnp.log(lax.optimization_barrier(jnp.sum(jnp.exp(logits - row_top[:, None]), axis=-1)))
        is_target = labels[:, None] == columns[None, :]
        target_logit = lax.optimization_barrier(jnp.sum(jnp.where(is_target, logits, 0.0), axis=-1))
        loss_total = loss_total + jnp.sum(scale_rows * (log_total - target_logit))
        logit_grad = (scale_rows[:, None] * (jnp.exp(logits - log_total[:, None]) - is_target.astype(jnp.float32))).astype(jnp.bfloat16)
        partial_grad = lax.dot_general(group_rows, logit_grad, (((0,), (0,)), ((), ())), preferred_element_type=jnp.float32)
        rounded = lax.optimization_barrier(partial_grad.astype(jnp.bfloat16))
        return ((grad_total + rounded.astype(jnp.float32), loss_total), None)
    start_state = (jnp.zeros((D, VOCAB), jnp.float32), jnp.zeros((), jnp.float32))
    final_state, ignored = lax.scan(one_group, start_state, (grouped, group_targets))
    return (final_state[0], final_state[1] / TOKENS)
```

```python
import jax
import jax.numpy as jnp
from jax import lax
from jax.experimental import pallas as pl
from jax.experimental.pallas import tpu as pltpu
from jax.sharding import PartitionSpec as P

norm_eps = 1e-05
MESH = pl.DeviceIdType.MESH
F32 = jnp.float32
BF16 = jnp.bfloat16
NZ, NX, NY = 16, 4, 4


def kernel(x_ref, u_ref, tgt_ref, scale_ref, gain_ref, o_ref, loss_ref,
           abuf, ubuf, acc, ssq, gbuf, tbuf, sta, stb, zst, lebuf, lbuf, pbuf, fin,
           r_o, r_d, r_c, q_o, q_d, q_c,
           swap_sem, ring_s, ring_r, sib_s, sib_r, u_s, u_r, u_loc, t_sem, st_sem, z_s, z_r, le_sem,
           g_sem, l_s, l_r, rs_s, rs_r, qs_s, qs_r):
    dp = lax.axis_index("dp")
    vo = lax.axis_index("vocab")
    c = dp % 2
    xl = (dp // 2) % 2
    y = dp // 4
    z = vo % NZ
    xh = vo // NZ
    x = xh * 2 + xl

    def dev(x_, y_, z_, c_):
        return ((y_ * 2 + x_ % 2) * 2 + c_, (x_ // 2) * NZ + z_)

    sibling = dev(x, y, z, 1 - c)
    partner = dev((x + 2) % 4, y, z, 1 - c)

    def rcopy(src, dst, s, r, to):
        return pltpu.make_async_remote_copy(src_ref=src, dst_ref=dst, send_sem=s, recv_sem=r,
                                            device_id=to, device_id_type=MESH)

    bar = pltpu.get_barrier_semaphore()

    def hello(to):
        pl.semaphore_signal(bar, inc=1, device_id=to, device_id_type=MESH)

    hello(sibling)
    hello(partner)

    def hello_z(k, carry):
        hello(dev(x, y, (z + k) % NZ, c))
        hello(dev((x + k % 4) % 4, (y + k // 4) % 4, z, c))
        return carry

    lax.fori_loop(1, 16, hello_z, 0)
    pl.semaphore_wait(bar, 32)

    mine = c == xh
    swap = rcopy(x_ref, abuf.at[1 - c, z], swap_sem.at[0], swap_sem.at[1], partner)
    swap_in = rcopy(x_ref, abuf.at[c, z], swap_sem.at[0], swap_sem.at[1], partner)

    def u_direct(k):
        j = (1 - xl) * 8 + k
        return rcopy(u_ref.at[pl.ds(2 * j, 2)], ubuf.at[pl.ds(2 * j, 2)], u_s.at[0, k], u_r.at[0, k], dev(3 - x, y, z, c))

    def u_direct_in(k):
        j = xl * 8 + k
        return rcopy(ubuf.at[pl.ds(2 * j, 2)], ubuf.at[pl.ds(2 * j, 2)], u_s.at[0, k], u_r.at[0, k], dev(3 - x, y, z, c))

    def u_mate(k):
        j = xl * 8 + k
        return rcopy(ubuf.at[pl.ds(2 * j, 2)], ubuf.at[pl.ds(2 * j, 2)], u_s.at[1, k], u_r.at[1, k], dev(xh * 2 + 1 - xl, y, z, c))

    def u_mate_in(k):
        j = (1 - xl) * 8 + k
        return rcopy(ubuf.at[pl.ds(2 * j, 2)], ubuf.at[pl.ds(2 * j, 2)], u_s.at[1, k], u_r.at[1, k], dev(xh * 2 + 1 - xl, y, z, c))

    u_local = pltpu.make_async_copy(u_ref, ubuf, u_loc)

    @pl.when(jnp.logical_not(mine))
    def _():
        swap.start()

    t_copy = rcopy(tgt_ref, tbuf, t_sem.at[0], t_sem.at[1], sibling)
    t_copy.start()

    @pl.when(mine)
    def _():
        abuf[c, z] = x_ref[...]
        u_local.start()

        def send_u(k, carry):
            u_direct(k).start()
            return carry

        lax.fori_loop(0, 8, send_u, 0)

    @pl.when(jnp.logical_not(mine))
    def _():
        swap_in.wait_recv()

    def step_slot(d, i):
        return (z - i + NZ) % NZ if d == 0 else (z + i) % NZ

    def half(slot, h):
        return abuf.at[c, slot, pl.ds(256 * h, 256)]

    def ring(d, h, i):
        ref = half(step_slot(d, i - 1), h)
        to = dev(x, y, (z + 1) % NZ, c) if d == 0 else dev(x, y, (z + NZ - 1) % NZ, c)
        return rcopy(ref, ref, ring_s.at[d, h, i - 1], ring_r.at[d, h, i - 1], to)

    def ring_in(d, h, i):
        ref = half(step_slot(d, i), h)
        to = dev(x, y, (z + 1) % NZ, c) if d == 0 else dev(x, y, (z + NZ - 1) % NZ, c)
        return rcopy(ref, ref, ring_s.at[d, h, i - 1], ring_r.at[d, h, i - 1], to)

    def sib(n, slot, h):
        ref = half(slot, h)
        return rcopy(ref, ref, sib_s.at[n, h], sib_r.at[n, h], sibling)

    def sib_in(n, slot, h):
        ref = abuf.at[1 - c, slot, pl.ds(256 * h, 256)]
        return rcopy(ref, ref, sib_s.at[n, h], sib_r.at[n, h], sibling)

    for h in range(2):
        for d in range(2):
            ring(d, h, 1).start()
    for h in range(2):
        sib(0, z, h).start()

    acc[...] = jnp.zeros_like(acc)
    ssq[...] = jnp.zeros_like(ssq)

    def ring_step(i, more):
        for h in range(2):
            for d in range(2):
                ring_in(d, h, i).wait_recv()
                if more == 2 or (more == 1 and h == d):
                    ring(d, h, i + 1).start()
                sib(2 * i - d, step_slot(d, i), h).start()

    def block_slot(n):
        off = jnp.where(n % 2 == 1, (n + 1) // 2, NZ - n // 2)
        return (z + off) % NZ

    def blocks(n, carry):
        slot = block_slot(n)
        for h in range(2):
            sib_in(n, slot, h).wait_recv()
        for cs in range(2):
            s = cs * NZ + slot
            a = abuf[cs, slot].astype(F32)
            ssq[...] += a[:, :128] * a[:, :128] + a[:, 128:] * a[:, 128:]
            ag = (a * gain_ref[pl.ds(s, 1), :]).astype(BF16)
            acc[...] += lax.dot_general(ubuf[s], ag, (((0,), (1,)), ((), ())), preferred_element_type=F32)
        return carry

    def loop_step(i, carry):
        ring_step(i, 2)

        @pl.when(jnp.logical_not(mine))
        def _():
            for k in range(2):
                u_direct_in(2 * (i - 1) + k).wait_recv()
                u_mate(2 * (i - 1) + k).start()
        return carry

    lax.fori_loop(1, 5, loop_step, 0)
    ring_step(5, 2)

    @pl.when(jnp.logical_not(mine))
    def _():
        def wait_u(k, carry):
            u_mate_in(k).wait_recv()
            return carry

        lax.fori_loop(0, 8, wait_u, 0)

    @pl.when(mine)
    def _():
        u_local.wait()

    lax.fori_loop(0, 5, blocks, 0)
    ring_step(6, 2)
    lax.fori_loop(5, 10, blocks, 0)
    ring_step(7, 1)
    lax.fori_loop(10, 13, blocks, 0)
    for d in range(2):
        ring_in(d, d, 8).wait_recv()
        sib(15, (z + 8) % NZ, d).start()
    lax.fori_loop(13, 16, blocks, 0)

    mean_sq = jnp.sum(ssq[...].T, axis=0, keepdims=True) * (1.0 / 8192.0)
    r_row = lax.rsqrt(mean_sq + norm_eps)
    logits = acc[...] * r_row
    acc[...] = logits
    t_copy.wait_recv()
    tgt = jnp.where(mine, tgt_ref[0:1, :], tbuf[0:1, :])
    ids = (((c * NZ + z) * 256) + lax.broadcasted_iota(jnp.int32, (256, 512), 0)).astype(F32)
    is_target = ids == tgt
    m = jnp.max(logits, axis=0, keepdims=True)
    sta[0:1, :] = m
    sta[1:2, :] = jnp.sum(jnp.exp(logits - m), axis=0, keepdims=True)
    sta[2:3, :] = jnp.sum(jnp.where(is_target, logits, 0.0), axis=0, keepdims=True)
    st_copy = rcopy(sta, stb, st_sem.at[0], st_sem.at[1], sibling)
    st_copy.start()
    st_copy.wait_recv()
    cols = pl.ds(pl.multiple_of(c * 256, 256), 256)
    m_a, m_b = sta[0:1, cols], stb[0:1, cols]
    m2 = jnp.maximum(m_a, m_b)
    s2 = sta[1:2, cols] * jnp.exp(m_a - m2) + stb[1:2, cols] * jnp.exp(m_b - m2)
    t2 = sta[2:3, cols] + stb[2:3, cols]
    zst[z] = jnp.concatenate(
        [m2[:, :128], m2[:, 128:], s2[:, :128], s2[:, 128:], t2[:, :128], t2[:, 128:], t2[:, :128], t2[:, 128:]], axis=0)

    def z_copy(k):
        return rcopy(zst.at[z], zst.at[z], z_s.at[k], z_r.at[k], dev(x, y, (z + k) % NZ, c))

    def z_in(k):
        slot = (z + NZ - k) % NZ
        return rcopy(zst.at[slot], zst.at[slot], z_s.at[k], z_r.at[k], dev(x, y, (z + k) % NZ, c))

    def z_start(k, carry):
        z_copy(k).start()
        return carry

    def z_wait(k, carry):
        z_in(k).wait_recv()
        return carry

    lax.fori_loop(1, NZ, z_start, 0)
    lax.fori_loop(1, NZ, z_wait, 0)
    st = zst[...]
    m16, s16, t16 = st[:, 0:2, :], st[:, 2:4, :], st[:, 4:6, :]
    top = jnp.max(m16, axis=0)
    lse = top + jnp.log(jnp.sum(s16 * jnp.exp(m16 - top[None]), axis=0))
    t_all = jnp.sum(t16, axis=0)
    lebuf[c] = jnp.concatenate([lse, t_all, lse, t_all], axis=0)
    le_copy = rcopy(lebuf.at[c], lebuf.at[c], le_sem.at[0], le_sem.at[1], sibling)
    le_in = rcopy(lebuf.at[1 - c], lebuf.at[1 - c], le_sem.at[0], le_sem.at[1], sibling)
    le_copy.start()
    le_in.wait_recv()
    lse_row = jnp.concatenate([lebuf[0, 0:1, :], lebuf[0, 1:2, :], lebuf[1, 0:1, :], lebuf[1, 1:2, :]], axis=1)
    t_row = jnp.concatenate([lebuf[0, 2:3, :], lebuf[0, 3:4, :], lebuf[1, 2:3, :], lebuf[1, 3:4, :]], axis=1)
    scale_row = scale_ref[0:1, :]
    grad = (scale_row * r_row) * (jnp.exp(acc[...] - lse_row) - is_target.astype(F32))
    gbuf[c] = grad.astype(BF16)
    g_copy = rcopy(gbuf.at[c], gbuf.at[c], g_sem.at[0], g_sem.at[1], sibling)
    g_in = rcopy(gbuf.at[1 - c], gbuf.at[1 - c], g_sem.at[0], g_sem.at[1], sibling)
    g_copy.start()

    loss4 = scale_row * (lse_row - t_row)
    loss1 = loss4[:, :128] + loss4[:, 128:256] + loss4[:, 256:384] + loss4[:, 384:]
    me = y * 4 + x
    lbuf[me] = jnp.broadcast_to(loss1, (8, 128))

    def l_copy(k):
        return rcopy(lbuf.at[me], lbuf.at[me], l_s.at[k], l_r.at[k], dev((x + k % 4) % 4, (y + k // 4) % 4, z, c))

    def l_in(k):
        slot = (y + 4 - k // 4) % 4 * 4 + (x + 4 - k % 4) % 4
        return rcopy(lbuf.at[slot], lbuf.at[slot], l_s.at[k], l_r.at[k], dev((x + k % 4) % 4, (y + k // 4) % 4, z, c))

    def l_start(k, carry):
        l_copy(k).start()
        return carry

    def l_wait(k, carry):
        l_in(k).wait_recv()
        l_copy(k).wait_send()
        return carry

    g_in.wait_recv()

    def along(axis, step):
        if axis == 0:
            return dev((x + step) % 4, y, z, c)
        return dev(x, (y + step) % 4, z, c)

    def grad_block(dy, dx):
        y_, x_ = (y + dy) % 4, (x + dx) % 4
        s = ((y_ * 2 + x_ % 2) * 2 + c) * 2
        plane, slot = s // NZ, s % NZ
        for k in range(2):
            pbuf[y_, x_, :, 256 * k:256 * k + 256] = jnp.dot(
                gbuf[x_ // 2], abuf[plane, slot + k], preferred_element_type=F32).astype(BF16)

    def blk(axis, step, o):
        if axis == 0:
            return pbuf.at[(y + o) % 4, (x + step) % 4]
        return pbuf.at[(y + step) % 4, (x + o) % 4]

    def part(axis, which):
        return pl.ds(128 * axis + 64 * which, 64)

    STEP = (1, 3)

    def send_o(axis, d, o):
        return rcopy(blk(axis, 2, o).at[part(axis, d)], r_o.at[axis, d, o], rs_s.at[0, axis, d, o], rs_r.at[0, axis, d, o], along(axis, STEP[d]))

    def send_d(axis, d, o):
        return rcopy(blk(axis, STEP[d], o).at[part(axis, 1 - d)], r_d.at[axis, d, o], rs_s.at[1, axis, d, o], rs_r.at[1, axis, d, o], along(axis, STEP[d]))

    def send_c(axis, d, o):
        return rcopy(blk(axis, STEP[d], o).at[part(axis, d)], r_c.at[axis, d, o], rs_s.at[2, axis, d, o], rs_r.at[2, axis, d, o], along(axis, STEP[d]))

    def send_o2(axis, d):
        return rcopy(blk(axis, 0, 2).at[part(axis, d)], q_o.at[axis, d], qs_s.at[0, axis, d], qs_r.at[0, axis, d], along(1 - axis, STEP[d]))

    def send_d2(axis, d):
        return rcopy(blk(axis, 0, STEP[d]).at[part(axis, 1 - d)], q_d.at[axis, d], qs_s.at[1, axis, d], qs_r.at[1, axis, d], along(1 - axis, STEP[d]))

    def send_c2(axis, d):
        return rcopy(blk(axis, 0, STEP[d]).at[part(axis, d)], q_c.at[axis, d], qs_s.at[2, axis, d], qs_r.at[2, axis, d], along(1 - axis, STEP[d]))

    def start_o(axis, o):
        for d in range(2):
            send_o(axis, d, o).start()

    def start_d(axis, o):
        for d in range(2):
            send_d(axis, d, o).start()

    ORDER = (2, 1, 3, 0)
    grad_block(2, 2)
    start_o(0, 2)
    start_o(1, 2)

    def o_blocks(k, carry):
        o = k
        grad_block(o, 2)
        start_o(0, o)
        grad_block(2, o)
        start_o(1, o)
        return carry

    o_blocks(1, 0)
    o_blocks(3, 0)
    o_blocks(0, 0)
    start_d(0, 2)
    start_d(1, 2)
    for dy in (1, 3):
        for dx in (1, 3):
            grad_block(dy, dx)
    for o in (1, 3):
        start_d(0, o)
        start_d(1, o)
    for dd in (1, 3):
        grad_block(0, dd)
        grad_block(dd, 0)
    start_d(0, 0)
    start_d(1, 0)
    grad_block(0, 0)
    lax.fori_loop(1, 16, l_start, 0)

    for o in ORDER:
        for axis in range(2):
            for d in range(2):
                send_o(axis, d, o).wait_recv()
                ref = blk(axis, STEP[d], o)
                rows = part(axis, d)
                ref[rows, :] = (ref[rows, :].astype(F32) + r_o[axis, d, o].astype(F32)).astype(BF16)
                send_c(axis, d, o).start()

    for o in ORDER:
        for axis in range(2):
            own = blk(axis, 0, o)
            for w in range(2):
                send_c(axis, w, o).wait_recv()
                send_d(axis, 1 - w, o).wait_recv()
                rows = part(axis, w)
                total = own[rows, :].astype(F32) + r_c[axis, w, o].astype(F32) + r_d[axis, 1 - w, o].astype(F32)
                if o == 0:
                    fin[rows, :] = total
                else:
                    own[rows, :] = total.astype(BF16)
            if o == 2:
                for d in range(2):
                    send_o2(axis, d).start()
            if o in STEP:
                send_d2(axis, STEP.index(o)).start()

    for axis in range(2):
        for d in range(2):
            send_o2(axis, d).wait_recv()
            ref = blk(axis, 0, STEP[d])
            rows = part(axis, d)
            ref[rows, :] = (ref[rows, :].astype(F32) + q_o[axis, d].astype(F32)).astype(BF16)
            send_c2(axis, d).start()

    s_own = ((y * 2 + xl) * 2 + c) * 2
    gain_own = jnp.concatenate([gain_ref[pl.ds(s_own, 1), :], gain_ref[pl.ds(s_own + 1, 1), :]], axis=1)
    for axis in range(2):
        for w in range(2):
            send_c2(axis, w).wait_recv()
            send_d2(axis, 1 - w).wait_recv()
            rows = part(axis, w)
            o_ref[rows, :] = (fin[rows, :] + q_c[axis, w].astype(F32) + q_d[axis, 1 - w].astype(F32)) * gain_own

    lax.fori_loop(1, 16, l_wait, 0)
    tot = jnp.sum(lbuf[...], axis=0)
    loss_ref[...] = jnp.broadcast_to(jnp.sum(tot, axis=1, keepdims=True) * (1.0 / 4096.0), (8, 128))

    for axis in range(2):
        for d in range(2):
            for o in range(4):
                send_o(axis, d, o).wait_send()
                send_d(axis, d, o).wait_send()
                send_c(axis, d, o).wait_send()
            send_o2(axis, d).wait_send()
            send_d2(axis, d).wait_send()
            send_c2(axis, d).wait_send()
    for copy in (t_copy, st_copy, le_copy, g_copy):
        copy.wait_send()

    def z_done(k, carry):
        z_copy(k).wait_send()
        return carry

    lax.fori_loop(1, NZ, z_done, 0)

    def ring_done(i, carry):
        for h in range(2):
            for d in range(2):
                ring(d, h, i).wait_send()
        return carry

    lax.fori_loop(1, 8, ring_done, 0)
    for d in range(2):
        ring(d, d, 8).wait_send()

    def sib_done(n, carry):
        for h in range(2):
            sib(n, block_slot(n), h).wait_send()
        return carry

    lax.fori_loop(0, 16, sib_done, 0)

    @pl.when(mine)
    def _():
        def done(k, carry):
            u_direct(k).wait_send()
            return carry

        lax.fori_loop(0, 8, done, 0)

    @pl.when(jnp.logical_not(mine))
    def _():
        swap.wait_send()

        def done(k, carry):
            u_mate(k).wait_send()
            return carry

        lax.fori_loop(0, 8, done, 0)


def per_device(hidden_states, exit_layers, targets, norm_gain, exit_scale, unembedding):
    layers, tok_count, local_width = hidden_states.shape
    exit_count = exit_layers.shape[1]
    row_len = tok_count // exit_layers.shape[0]
    row_layers = jnp.repeat(exit_layers, row_len, axis=0)
    layer_match = row_layers.T[:, None, :] == jnp.arange(layers, dtype=jnp.int32)[None, :, None]
    selected = jnp.sum(
        jnp.where(layer_match[..., None], hidden_states[None].astype(F32), 0.0), axis=1
    ).astype(BF16).reshape(exit_count * tok_count, local_width)
    tgt = jnp.broadcast_to(jnp.tile(targets, exit_count).astype(F32)[None], (8, 512))
    scale = jnp.broadcast_to(jnp.repeat(exit_scale, tok_count)[None], (8, 512))
    gain = norm_gain.astype(F32).reshape(32, 256)
    vmem = pl.BlockSpec(memory_space=pltpu.VMEM)
    dma = pltpu.SemaphoreType.DMA
    grad_t, loss = pl.pallas_call(
        kernel,
        out_shape=(jax.ShapeDtypeStruct((256, 512), F32), jax.ShapeDtypeStruct((8, 128), F32)),
        in_specs=[vmem, pl.BlockSpec(memory_space=pl.ANY), vmem, vmem, vmem],
        out_specs=(vmem, vmem),
        scratch_shapes=[
            pltpu.VMEM((2, 16, 512, 256), BF16),
            pltpu.VMEM((32, 256, 256), BF16),
            pltpu.VMEM((256, 512), F32),
            pltpu.VMEM((512, 128), F32),
            pltpu.VMEM((2, 256, 512), BF16),
            pltpu.VMEM((8, 512), F32),
            pltpu.VMEM((8, 512), F32),
            pltpu.VMEM((8, 512), F32),
            pltpu.VMEM((16, 8, 128), F32),
            pltpu.VMEM((2, 8, 128), F32),
            pltpu.VMEM((16, 8, 128), F32),
            pltpu.VMEM((4, 4, 256, 512), BF16),
            pltpu.VMEM((256, 512), F32),
            pltpu.VMEM((2, 2, 4, 64, 512), BF16),
            pltpu.VMEM((2, 2, 4, 64, 512), BF16),
            pltpu.VMEM((2, 2, 4, 64, 512), BF16),
            pltpu.VMEM((2, 2, 64, 512), BF16),
            pltpu.VMEM((2, 2, 64, 512), BF16),
            pltpu.VMEM((2, 2, 64, 512), BF16),
            dma((2,)), dma((2, 2, 8)), dma((2, 2, 8)), dma((16, 2)), dma((16, 2)),
            dma((2, 8)), dma((2, 8)), dma, dma((2,)), dma((2,)), dma((16,)), dma((16,)), dma((2,)),
            dma((2,)), dma((16,)), dma((16,)), dma((3, 2, 2, 4)), dma((3, 2, 2, 4)), dma((3, 2, 2)), dma((3, 2, 2)),
        ],
        compiler_params=pltpu.CompilerParams(
            collective_id=0, has_side_effects=True, vmem_limit_bytes=56 << 20),
    )(selected, unembedding.reshape(32, 256, 256), tgt, scale, gain)
    return (grad_t.T, loss[0, 0])


def solution(mesh):
    in_specs = (P(None, "dp", "vocab"), P("dp", None), P("dp"), P(), P(), P(None, "vocab"))
    out_specs = (P("dp", "vocab"), P())
    return jax.shard_map(
        per_device, mesh=mesh, in_specs=in_specs, out_specs=out_specs, check_vma=False
    )
```

```python
import jax
import jax.numpy as jnp
from jax import lax
from jax.experimental import pallas as pl
from jax.experimental.pallas import tpu as pltpu
from jax.sharding import PartitionSpec as P

norm_eps = 1e-05
MESH = pl.DeviceIdType.MESH
F32 = jnp.float32
BF16 = jnp.bfloat16
NZ, NX, NY = 16, 4, 4


def kernel(el_ref, scale_ref, hid_ref, u_ref, tgt_ref, gain_ref, o_ref, loss_ref,
           hbuf, xbuf, tsrc, gain, in_sem, abuf, ubuf, acc, ssq, gbuf, tbuf, sta, stb, zst, lebuf, lbuf, pbuf, fin,
           r_o, r_d, r_c, q_o, q_d, q_c,
           swap_sem, ring_s, ring_r, sib_s, sib_r, u_s, u_r, u_loc, t_sem, st_sem, z_s, z_r, le_sem,
           g_sem, l_s, l_r, rs_s, rs_r, qs_s, qs_r):
    dp = lax.axis_index("dp")
    vo = lax.axis_index("vocab")
    c = dp % 2
    xl = (dp // 2) % 2
    y = dp // 4
    z = vo % NZ
    xh = vo // NZ
    x = xh * 2 + xl

    def dev(x_, y_, z_, c_):
        return ((y_ * 2 + x_ % 2) * 2 + c_, (x_ // 2) * NZ + z_)

    sibling = dev(x, y, z, 1 - c)
    partner = dev((x + 2) % 4, y, z, 1 - c)

    def rcopy(src, dst, s, r, to):
        return pltpu.make_async_remote_copy(src_ref=src, dst_ref=dst, send_sem=s, recv_sem=r,
                                            device_id=to, device_id_type=MESH)

    hid_copy = pltpu.make_async_copy(hid_ref, hbuf, in_sem)
    hid_copy.start()

    bar = pltpu.get_barrier_semaphore()

    def hello(to):
        pl.semaphore_signal(bar, inc=1, device_id=to, device_id_type=MESH)

    hello(sibling)
    hello(partner)

    def hello_z(k, carry):
        hello(dev(x, y, (z + k) % NZ, c))
        hello(dev((x + k % 4) % 4, (y + k // 4) % 4, z, c))
        return carry

    lax.fori_loop(1, 16, hello_z, 0)

    def select(dst):
        for e in range(2):
            for row in range(4):
                dst[pl.ds(256 * e + 64 * row, 64), :] = hbuf[el_ref[e, row], pl.ds(64 * row, 64), :]

    mine = c == xh
    hid_copy.wait()

    @pl.when(mine)
    def _():
        select(abuf.at[c, z])

    @pl.when(jnp.logical_not(mine))
    def _():
        select(xbuf)

    pl.semaphore_wait(bar, 32)

    swap = rcopy(xbuf, abuf.at[1 - c, z], swap_sem.at[0], swap_sem.at[1], partner)
    swap_in = rcopy(xbuf, abuf.at[c, z], swap_sem.at[0], swap_sem.at[1], partner)

    def u_direct(k):
        j = (1 - xl) * 8 + k
        return rcopy(u_ref.at[pl.ds(2 * j, 2)], ubuf.at[pl.ds(2 * j, 2)], u_s.at[0, k], u_r.at[0, k], dev(3 - x, y, z, c))

    def u_direct_in(k):
        j = xl * 8 + k
        return rcopy(ubuf.at[pl.ds(2 * j, 2)], ubuf.at[pl.ds(2 * j, 2)], u_s.at[0, k], u_r.at[0, k], dev(3 - x, y, z, c))

    def u_mate(k):
        j = xl * 8 + k
        return rcopy(ubuf.at[pl.ds(2 * j, 2)], ubuf.at[pl.ds(2 * j, 2)], u_s.at[1, k], u_r.at[1, k], dev(xh * 2 + 1 - xl, y, z, c))

    def u_mate_in(k):
        j = (1 - xl) * 8 + k
        return rcopy(ubuf.at[pl.ds(2 * j, 2)], ubuf.at[pl.ds(2 * j, 2)], u_s.at[1, k], u_r.at[1, k], dev(xh * 2 + 1 - xl, y, z, c))

    u_local = pltpu.make_async_copy(u_ref, ubuf, u_loc)

    @pl.when(jnp.logical_not(mine))
    def _():
        swap.start()

    tsrc[0:2, :] = tgt_ref[...].astype(F32)
    t_copy = rcopy(tsrc, tbuf, t_sem.at[0], t_sem.at[1], sibling)
    t_copy.start()

    @pl.when(mine)
    def _():
        u_local.start()

        def send_u(k, carry):
            u_direct(k).start()
            return carry

        lax.fori_loop(0, 8, send_u, 0)

    @pl.when(jnp.logical_not(mine))
    def _():
        swap_in.wait_recv()

    def step_slot(d, i):
        return (z - i + NZ) % NZ if d == 0 else (z + i) % NZ

    def half(slot, h):
        return abuf.at[c, slot, pl.ds(256 * h, 256)]

    def ring(d, h, i):
        ref = half(step_slot(d, i - 1), h)
        to = dev(x, y, (z + 1) % NZ, c) if d == 0 else dev(x, y, (z + NZ - 1) % NZ, c)
        return rcopy(ref, ref, ring_s.at[d, h, i - 1], ring_r.at[d, h, i - 1], to)

    def ring_in(d, h, i):
        ref = half(step_slot(d, i), h)
        to = dev(x, y, (z + 1) % NZ, c) if d == 0 else dev(x, y, (z + NZ - 1) % NZ, c)
        return rcopy(ref, ref, ring_s.at[d, h, i - 1], ring_r.at[d, h, i - 1], to)

    def sib(n, slot, h):
        ref = half(slot, h)
        return rcopy(ref, ref, sib_s.at[n, h], sib_r.at[n, h], sibling)

    def sib_in(n, slot, h):
        ref = abuf.at[1 - c, slot, pl.ds(256 * h, 256)]
        return rcopy(ref, ref, sib_s.at[n, h], sib_r.at[n, h], sibling)

    for h in range(2):
        for d in range(2):
            ring(d, h, 1).start()
    for h in range(2):
        sib(0, z, h).start()

    gain[...] = gain_ref[...].astype(F32)

    def gain_row(s):
        return jnp.concatenate([gain[pl.ds(2 * s, 1), :], gain[pl.ds(2 * s + 1, 1), :]], axis=1)

    acc[...] = jnp.zeros_like(acc)
    ssq[...] = jnp.zeros_like(ssq)

    def ring_step(i, more):
        for h in range(2):
            for d in range(2):
                ring_in(d, h, i).wait_recv()
                if more == 2 or (more == 1 and h == d):
                    ring(d, h, i + 1).start()
                sib(2 * i - d, step_slot(d, i), h).start()

    def block_slot(n):
        off = jnp.where(n % 2 == 1, (n + 1) // 2, NZ - n // 2)
        return (z + off) % NZ

    def blocks(n, carry):
        slot = block_slot(n)
        for h in range(2):
            sib_in(n, slot, h).wait_recv()
        for cs in range(2):
            s = cs * NZ + slot
            a = abuf[cs, slot].astype(F32)
            ssq[...] += a[:, :128] * a[:, :128] + a[:, 128:] * a[:, 128:]
            ag = (a * gain_row(s)).astype(BF16)
            acc[...] += lax.dot_general(ubuf[s], ag, (((0,), (1,)), ((), ())), preferred_element_type=F32)
        return carry

    def loop_step(i, carry):
        ring_step(i, 2)

        @pl.when(jnp.logical_not(mine))
        def _():
            for k in range(2):
                u_direct_in(2 * (i - 1) + k).wait_recv()
                u_mate(2 * (i - 1) + k).start()
        return carry

    lax.fori_loop(1, 5, loop_step, 0)
    ring_step(5, 2)

    @pl.when(jnp.logical_not(mine))
    def _():
        def wait_u(k, carry):
            u_mate_in(k).wait_recv()
            return carry

        lax.fori_loop(0, 8, wait_u, 0)

    @pl.when(mine)
    def _():
        u_local.wait()

    lax.fori_loop(0, 5, blocks, 0)
    ring_step(6, 2)
    lax.fori_loop(5, 10, blocks, 0)
    ring_step(7, 1)
    lax.fori_loop(10, 13, blocks, 0)
    for d in range(2):
        ring_in(d, d, 8).wait_recv()
        sib(15, (z + 8) % NZ, d).start()
    lax.fori_loop(13, 16, blocks, 0)

    mean_sq = jnp.sum(ssq[...].T, axis=0, keepdims=True) * (1.0 / 8192.0)
    r_row = lax.rsqrt(mean_sq + norm_eps)
    logits = acc[...] * r_row
    acc[...] = logits
    t_copy.wait_recv()
    t2x = jnp.where(mine, tsrc[0:2, :], tbuf[0:2, :])
    tgt = jnp.concatenate([t2x[0:1, :], t2x[1:2, :], t2x[0:1, :], t2x[1:2, :]], axis=1)
    ids = (((c * NZ + z) * 256) + lax.broadcasted_iota(jnp.int32, (256, 512), 0)).astype(F32)
    is_target = ids == tgt
    m = jnp.max(logits, axis=0, keepdims=True)
    sta[0:1, :] = m
    sta[1:2, :] = jnp.sum(jnp.exp(logits - m), axis=0, keepdims=True)
    sta[2:3, :] = jnp.sum(jnp.where(is_target, logits, 0.0), axis=0, keepdims=True)
    st_copy = rcopy(sta, stb, st_sem.at[0], st_sem.at[1], sibling)
    st_copy.start()
    st_copy.wait_recv()
    cols = pl.ds(pl.multiple_of(c * 256, 256), 256)
    m_a, m_b = sta[0:1, cols], stb[0:1, cols]
    m2 = jnp.maximum(m_a, m_b)
    s2 = sta[1:2, cols] * jnp.exp(m_a - m2) + stb[1:2, cols] * jnp.exp(m_b - m2)
    t2 = sta[2:3, cols] + stb[2:3, cols]
    zst[z] = jnp.concatenate(
        [m2[:, :128], m2[:, 128:], s2[:, :128], s2[:, 128:], t2[:, :128], t2[:, 128:], t2[:, :128], t2[:, 128:]], axis=0)

    def z_copy(k):
        return rcopy(zst.at[z], zst.at[z], z_s.at[k], z_r.at[k], dev(x, y, (z + k) % NZ, c))

    def z_in(k):
        slot = (z + NZ - k) % NZ
        return rcopy(zst.at[slot], zst.at[slot], z_s.at[k], z_r.at[k], dev(x, y, (z + k) % NZ, c))

    def z_start(k, carry):
        z_copy(k).start()
        return carry

    def z_wait(k, carry):
        z_in(k).wait_recv()
        return carry

    lax.fori_loop(1, NZ, z_start, 0)
    lax.fori_loop(1, NZ, z_wait, 0)
    st = zst[...]
    m16, s16, t16 = st[:, 0:2, :], st[:, 2:4, :], st[:, 4:6, :]
    top = jnp.max(m16, axis=0)
    lse = top + jnp.log(jnp.sum(s16 * jnp.exp(m16 - top[None]), axis=0))
    t_all = jnp.sum(t16, axis=0)
    lebuf[c] = jnp.concatenate([lse, t_all, lse, t_all], axis=0)
    le_copy = rcopy(lebuf.at[c], lebuf.at[c], le_sem.at[0], le_sem.at[1], sibling)
    le_in = rcopy(lebuf.at[1 - c], lebuf.at[1 - c], le_sem.at[0], le_sem.at[1], sibling)
    le_copy.start()
    le_in.wait_recv()
    lse_row = jnp.concatenate([lebuf[0, 0:1, :], lebuf[0, 1:2, :], lebuf[1, 0:1, :], lebuf[1, 1:2, :]], axis=1)
    t_row = jnp.concatenate([lebuf[0, 2:3, :], lebuf[0, 3:4, :], lebuf[1, 2:3, :], lebuf[1, 3:4, :]], axis=1)
    scale_row = jnp.where(lax.broadcasted_iota(jnp.int32, (1, 512), 1) < 256, scale_ref[0], scale_ref[1])
    grad = (scale_row * r_row) * (jnp.exp(acc[...] - lse_row) - is_target.astype(F32))
    gbuf[c] = grad.astype(BF16)
    g_copy = rcopy(gbuf.at[c], gbuf.at[c], g_sem.at[0], g_sem.at[1], sibling)
    g_in = rcopy(gbuf.at[1 - c], gbuf.at[1 - c], g_sem.at[0], g_sem.at[1], sibling)
    g_copy.start()

    loss4 = scale_row * (lse_row - t_row)
    loss1 = loss4[:, :128] + loss4[:, 128:256] + loss4[:, 256:384] + loss4[:, 384:]
    me = y * 4 + x
    lbuf[me] = jnp.broadcast_to(loss1, (8, 128))

    def l_copy(k):
        return rcopy(lbuf.at[me], lbuf.at[me], l_s.at[k], l_r.at[k], dev((x + k % 4) % 4, (y + k // 4) % 4, z, c))

    def l_in(k):
        slot = (y + 4 - k // 4) % 4 * 4 + (x + 4 - k % 4) % 4
        return rcopy(lbuf.at[slot], lbuf.at[slot], l_s.at[k], l_r.at[k], dev((x + k % 4) % 4, (y + k // 4) % 4, z, c))

    def l_start(k, carry):
        l_copy(k).start()
        return carry

    def l_wait(k, carry):
        l_in(k).wait_recv()
        l_copy(k).wait_send()
        return carry

    g_in.wait_recv()

    def along(axis, step):
        if axis == 0:
            return dev((x + step) % 4, y, z, c)
        return dev(x, (y + step) % 4, z, c)

    def grad_block(dy, dx):
        y_, x_ = (y + dy) % 4, (x + dx) % 4
        s = ((y_ * 2 + x_ % 2) * 2 + c) * 2
        plane, slot = s // NZ, s % NZ
        for k in range(2):
            pbuf[y_, x_, :, 256 * k:256 * k + 256] = jnp.dot(
                gbuf[x_ // 2], abuf[plane, slot + k], preferred_element_type=F32).astype(BF16)

    def blk(axis, step, o):
        if axis == 0:
            return pbuf.at[(y + o) % 4, (x + step) % 4]
        return pbuf.at[(y + step) % 4, (x + o) % 4]

    def part(axis, which):
        return pl.ds(128 * axis + 64 * which, 64)

    STEP = (1, 3)

    def send_o(axis, d, o):
        return rcopy(blk(axis, 2, o).at[part(axis, d)], r_o.at[axis, d, o], rs_s.at[0, axis, d, o], rs_r.at[0, axis, d, o], along(axis, STEP[d]))

    def send_d(axis, d, o):
        return rcopy(blk(axis, STEP[d], o).at[part(axis, 1 - d)], r_d.at[axis, d, o], rs_s.at[1, axis, d, o], rs_r.at[1, axis, d, o], along(axis, STEP[d]))

    def send_c(axis, d, o):
        return rcopy(blk(axis, STEP[d], o).at[part(axis, d)], r_c.at[axis, d, o], rs_s.at[2, axis, d, o], rs_r.at[2, axis, d, o], along(axis, STEP[d]))

    def send_o2(axis, d):
        return rcopy(blk(axis, 0, 2).at[part(axis, d)], q_o.at[axis, d], qs_s.at[0, axis, d], qs_r.at[0, axis, d], along(1 - axis, STEP[d]))

    def send_d2(axis, d):
        return rcopy(blk(axis, 0, STEP[d]).at[part(axis, 1 - d)], q_d.at[axis, d], qs_s.at[1, axis, d], qs_r.at[1, axis, d], along(1 - axis, STEP[d]))

    def send_c2(axis, d):
        return rcopy(blk(axis, 0, STEP[d]).at[part(axis, d)], q_c.at[axis, d], qs_s.at[2, axis, d], qs_r.at[2, axis, d], along(1 - axis, STEP[d]))

    def start_o(axis, o):
        for d in range(2):
            send_o(axis, d, o).start()

    def start_d(axis, o):
        for d in range(2):
            send_d(axis, d, o).start()

    ORDER = (2, 1, 3, 0)
    grad_block(2, 2)
    start_o(0, 2)
    start_o(1, 2)

    def o_blocks(k, carry):
        o = k
        grad_block(o, 2)
        start_o(0, o)
        grad_block(2, o)
        start_o(1, o)
        return carry

    o_blocks(1, 0)
    o_blocks(3, 0)
    o_blocks(0, 0)
    start_d(0, 2)
    start_d(1, 2)
    for dy in (1, 3):
        for dx in (1, 3):
            grad_block(dy, dx)
    for o in (1, 3):
        start_d(0, o)
        start_d(1, o)
    for dd in (1, 3):
        grad_block(0, dd)
        grad_block(dd, 0)
    start_d(0, 0)
    start_d(1, 0)
    grad_block(0, 0)
    lax.fori_loop(1, 16, l_start, 0)

    for o in ORDER:
        for axis in range(2):
            for d in range(2):
                send_o(axis, d, o).wait_recv()
                ref = blk(axis, STEP[d], o)
                rows = part(axis, d)
                ref[rows, :] = (ref[rows, :].astype(F32) + r_o[axis, d, o].astype(F32)).astype(BF16)
                send_c(axis, d, o).start()

    for o in ORDER:
        for axis in range(2):
            own = blk(axis, 0, o)
            for w in range(2):
                send_c(axis, w, o).wait_recv()
                send_d(axis, 1 - w, o).wait_recv()
                rows = part(axis, w)
                total = own[rows, :].astype(F32) + r_c[axis, w, o].astype(F32) + r_d[axis, 1 - w, o].astype(F32)
                if o == 0:
                    fin[rows, :] = total
                else:
                    own[rows, :] = total.astype(BF16)
            if o == 2:
                for d in range(2):
                    send_o2(axis, d).start()
            if o in STEP:
                send_d2(axis, STEP.index(o)).start()

    for axis in range(2):
        for d in range(2):
            send_o2(axis, d).wait_recv()
            ref = blk(axis, 0, STEP[d])
            rows = part(axis, d)
            ref[rows, :] = (ref[rows, :].astype(F32) + q_o[axis, d].astype(F32)).astype(BF16)
            send_c2(axis, d).start()

    s_own = ((y * 2 + xl) * 2 + c) * 2
    gain_own = jnp.concatenate([gain_row(s_own), gain_row(s_own + 1)], axis=1)
    for axis in range(2):
        for w in range(2):
            send_c2(axis, w).wait_recv()
            send_d2(axis, 1 - w).wait_recv()
            rows = part(axis, w)
            o_ref[rows, :] = (fin[rows, :] + q_c[axis, w].astype(F32) + q_d[axis, 1 - w].astype(F32)) * gain_own

    lax.fori_loop(1, 16, l_wait, 0)
    tot = jnp.sum(lbuf[...], axis=0)
    loss_ref[0] = jnp.sum(tot[0:1, :]) * (1.0 / 4096.0)

    for axis in range(2):
        for d in range(2):
            for o in range(4):
                send_o(axis, d, o).wait_send()
                send_d(axis, d, o).wait_send()
                send_c(axis, d, o).wait_send()
            send_o2(axis, d).wait_send()
            send_d2(axis, d).wait_send()
            send_c2(axis, d).wait_send()
    for copy in (t_copy, st_copy, le_copy, g_copy):
        copy.wait_send()

    def z_done(k, carry):
        z_copy(k).wait_send()
        return carry

    lax.fori_loop(1, NZ, z_done, 0)

    def ring_done(i, carry):
        for h in range(2):
            for d in range(2):
                ring(d, h, i).wait_send()
        return carry

    lax.fori_loop(1, 8, ring_done, 0)
    for d in range(2):
        ring(d, d, 8).wait_send()

    def sib_done(n, carry):
        for h in range(2):
            sib(n, block_slot(n), h).wait_send()
        return carry

    lax.fori_loop(0, 16, sib_done, 0)

    @pl.when(mine)
    def _():
        def done(k, carry):
            u_direct(k).wait_send()
            return carry

        lax.fori_loop(0, 8, done, 0)

    @pl.when(jnp.logical_not(mine))
    def _():
        swap.wait_send()

        def done(k, carry):
            u_mate(k).wait_send()
            return carry

        lax.fori_loop(0, 8, done, 0)


def per_device(hidden_states, exit_layers, targets, norm_gain, exit_scale, unembedding):
    vmem = pl.BlockSpec(memory_space=pltpu.VMEM)
    smem = pl.BlockSpec(memory_space=pltpu.SMEM)
    anywhere = pl.BlockSpec(memory_space=pl.ANY)
    dma = pltpu.SemaphoreType.DMA
    grad_t, loss = pl.pallas_call(
        kernel,
        out_shape=(jax.ShapeDtypeStruct((256, 512), F32), jax.ShapeDtypeStruct((1,), F32)),
        in_specs=[smem, smem, anywhere, anywhere, vmem, vmem],
        out_specs=(vmem, smem),
        scratch_shapes=[
            pltpu.VMEM((4, 256, 256), BF16),
            pltpu.VMEM((512, 256), BF16),
            pltpu.VMEM((8, 128), F32),
            pltpu.VMEM((64, 128), F32),
            dma,
            pltpu.VMEM((2, 16, 512, 256), BF16),
            pltpu.VMEM((32, 256, 256), BF16),
            pltpu.VMEM((256, 512), F32),
            pltpu.VMEM((512, 128), F32),
            pltpu.VMEM((2, 256, 512), BF16),
            pltpu.VMEM((8, 128), F32),
            pltpu.VMEM((8, 512), F32),
            pltpu.VMEM((8, 512), F32),
            pltpu.VMEM((16, 8, 128), F32),
            pltpu.VMEM((2, 8, 128), F32),
            pltpu.VMEM((16, 8, 128), F32),
            pltpu.VMEM((4, 4, 256, 512), BF16),
            pltpu.VMEM((256, 512), F32),
            pltpu.VMEM((2, 2, 4, 64, 512), BF16),
            pltpu.VMEM((2, 2, 4, 64, 512), BF16),
            pltpu.VMEM((2, 2, 4, 64, 512), BF16),
            pltpu.VMEM((2, 2, 64, 512), BF16),
            pltpu.VMEM((2, 2, 64, 512), BF16),
            pltpu.VMEM((2, 2, 64, 512), BF16),
            dma((2,)), dma((2, 2, 8)), dma((2, 2, 8)), dma((16, 2)), dma((16, 2)),
            dma((2, 8)), dma((2, 8)), dma, dma((2,)), dma((2,)), dma((16,)), dma((16,)), dma((2,)),
            dma((2,)), dma((16,)), dma((16,)), dma((3, 2, 2, 4)), dma((3, 2, 2, 4)), dma((3, 2, 2)), dma((3, 2, 2)),
        ],
        compiler_params=pltpu.CompilerParams(
            collective_id=0, has_side_effects=True, vmem_limit_bytes=56 << 20),
    )(exit_layers.T, exit_scale, hidden_states, unembedding.reshape(32, 256, 256),
      targets.reshape(2, 128), norm_gain.reshape(64, 128))
    return (grad_t.T, loss.reshape(()))


def solution(mesh):
    in_specs = (P(None, "dp", "vocab"), P("dp", None), P("dp"), P(), P(), P(None, "vocab"))
    out_specs = (P("dp", "vocab"), P())
    return jax.shard_map(
        per_device, mesh=mesh, in_specs=in_specs, out_specs=out_specs, check_vma=False
    )
```

```python
import jax
import jax.numpy as jnp
from jax import lax
from jax.experimental import pallas as pl
from jax.experimental.pallas import tpu as pltpu
from jax.sharding import PartitionSpec as P

norm_eps = 1e-05
MESH = pl.DeviceIdType.MESH
F32 = jnp.float32
BF16 = jnp.bfloat16
NZ, NX, NY = 16, 4, 4


def kernel(el_any, scale_any, hid_ref, u_ref, tgt_any, gain_any, o_ref, loss_ref,
           el_ref, scale_ref, tgt_ref, gain_ref, hbuf, xbuf, tsrc, gain, in_sem,
           abuf, ubuf, acc, accb, ssq, gbuf, tbuf, zst, zt, lebuf, tpair, lx, ly, pbuf, fin,
           r_o, r_d, r_c, q_o, q_d, q_c,
           swap_sem, ring_s, ring_r, sib_s, sib_r, u_s, u_r, u_loc, t_sem, lg_sem, z_s, z_r, zt_s, zt_r, le_sem,
           tp_sem, l_s, l_r, rs_s, rs_r, qs_s, qs_r):
    dp = lax.axis_index("dp")
    vo = lax.axis_index("vocab")
    c = dp % 2
    xl = (dp // 2) % 2
    y = dp // 4
    z = vo % NZ
    xh = vo // NZ
    x = xh * 2 + xl

    def dev(x_, y_, z_, c_):
        return ((y_ * 2 + x_ % 2) * 2 + c_, (x_ // 2) * NZ + z_)

    sibling = dev(x, y, z, 1 - c)
    partner = dev((x + 2) % 4, y, z, 1 - c)

    def rcopy(src, dst, s, r, to):
        return pltpu.make_async_remote_copy(src_ref=src, dst_ref=dst, send_sem=s, recv_sem=r,
                                            device_id=to, device_id_type=MESH)

    bar = pltpu.get_barrier_semaphore()
    for to in (sibling, partner, dev(x, y, (z + 1) % NZ, c), dev(x, y, (z + NZ - 1) % NZ, c)):
        pl.semaphore_signal(bar, inc=1, device_id=to, device_id_type=MESH)
    for k in range(1, 4):
        pl.semaphore_signal(bar, inc=1, device_id=dev((x + k) % 4, y, z, c), device_id_type=MESH)
        pl.semaphore_signal(bar, inc=1, device_id=dev(x, (y + k) % 4, z, c), device_id_type=MESH)

    inputs = [pltpu.make_async_copy(a, b, in_sem.at[k]) for k, (a, b) in enumerate((
        (hid_ref, hbuf), (el_any, el_ref), (scale_any, scale_ref), (tgt_any, tgt_ref), (gain_any, gain_ref)))]
    for copy in inputs:
        copy.start()

    def select(dst):
        for e in range(2):
            for row in range(4):
                dst[pl.ds(256 * e + 64 * row, 64), :] = hbuf[el_ref[e, row], pl.ds(64 * row, 64), :]

    mine = c == xh
    for copy in inputs:
        copy.wait()

    @pl.when(mine)
    def _():
        select(abuf.at[c, z])

    @pl.when(jnp.logical_not(mine))
    def _():
        select(xbuf)

    pl.semaphore_wait(bar, 10)

    swap = rcopy(xbuf, abuf.at[1 - c, z], swap_sem.at[0], swap_sem.at[1], partner)
    swap_in = rcopy(xbuf, abuf.at[c, z], swap_sem.at[0], swap_sem.at[1], partner)

    def u_direct(k):
        j = (1 - xl) * 8 + k
        return rcopy(u_ref.at[pl.ds(2 * j, 2)], ubuf.at[pl.ds(2 * j, 2)], u_s.at[0, k], u_r.at[0, k], dev(3 - x, y, z, c))

    def u_direct_in(k):
        j = xl * 8 + k
        return rcopy(ubuf.at[pl.ds(2 * j, 2)], ubuf.at[pl.ds(2 * j, 2)], u_s.at[0, k], u_r.at[0, k], dev(3 - x, y, z, c))

    def u_mate(k):
        j = xl * 8 + k
        return rcopy(ubuf.at[pl.ds(2 * j, 2)], ubuf.at[pl.ds(2 * j, 2)], u_s.at[1, k], u_r.at[1, k], dev(xh * 2 + 1 - xl, y, z, c))

    def u_mate_in(k):
        j = (1 - xl) * 8 + k
        return rcopy(ubuf.at[pl.ds(2 * j, 2)], ubuf.at[pl.ds(2 * j, 2)], u_s.at[1, k], u_r.at[1, k], dev(xh * 2 + 1 - xl, y, z, c))

    u_local = pltpu.make_async_copy(u_ref, ubuf, u_loc)

    @pl.when(jnp.logical_not(mine))
    def _():
        swap.start()

    tsrc[0:2, :] = tgt_ref[...].astype(F32)
    t_copy = rcopy(tsrc, tbuf, t_sem.at[0], t_sem.at[1], sibling)
    t_copy.start()

    @pl.when(mine)
    def _():
        u_local.start()

        def send_u(k, carry):
            u_direct(k).start()
            return carry

        lax.fori_loop(0, 8, send_u, 0)

    @pl.when(jnp.logical_not(mine))
    def _():
        swap_in.wait_recv()

    def step_slot(d, i):
        return (z - i + NZ) % NZ if d == 0 else (z + i) % NZ

    def half(slot, h):
        return abuf.at[c, slot, pl.ds(256 * h, 256)]

    def ring(d, h, i):
        ref = half(step_slot(d, i - 1), h)
        to = dev(x, y, (z + 1) % NZ, c) if d == 0 else dev(x, y, (z + NZ - 1) % NZ, c)
        return rcopy(ref, ref, ring_s.at[d, h, i - 1], ring_r.at[d, h, i - 1], to)

    def ring_in(d, h, i):
        ref = half(step_slot(d, i), h)
        to = dev(x, y, (z + 1) % NZ, c) if d == 0 else dev(x, y, (z + NZ - 1) % NZ, c)
        return rcopy(ref, ref, ring_s.at[d, h, i - 1], ring_r.at[d, h, i - 1], to)

    def sib(n, slot, h):
        ref = half(slot, h)
        return rcopy(ref, ref, sib_s.at[n, h], sib_r.at[n, h], sibling)

    def sib_in(n, slot, h):
        ref = abuf.at[1 - c, slot, pl.ds(256 * h, 256)]
        return rcopy(ref, ref, sib_s.at[n, h], sib_r.at[n, h], sibling)

    for h in range(2):
        for d in range(2):
            ring(d, h, 1).start()
    for h in range(2):
        sib(0, z, h).start()

    gain[...] = gain_ref[...].astype(F32)

    def gain_row(s):
        return jnp.concatenate([gain[pl.ds(2 * s, 1), :], gain[pl.ds(2 * s + 1, 1), :]], axis=1)

    acc[...] = jnp.zeros_like(acc)
    ssq[...] = jnp.zeros_like(ssq)

    def ring_step(i, more):
        for h in range(2):
            for d in range(2):
                ring_in(d, h, i).wait_recv()
                if more == 2 or (more == 1 and h == d):
                    ring(d, h, i + 1).start()
                sib(2 * i - d, step_slot(d, i), h).start()

    def block_slot(n):
        off = jnp.where(n % 2 == 1, (n + 1) // 2, NZ - n // 2)
        return (z + off) % NZ

    def blocks(n, carry):
        slot = block_slot(n)
        for h in range(2):
            sib_in(n, slot, h).wait_recv()
        for cs in range(2):
            s = cs * NZ + slot
            a = abuf[cs, slot].astype(F32)
            ssq[...] += a[:, :128] * a[:, :128] + a[:, 128:] * a[:, 128:]
            ag = (a * gain_row(s)).astype(BF16)
            acc[...] += lax.dot_general(ubuf[s], ag, (((0,), (1,)), ((), ())), preferred_element_type=F32)
        return carry

    def loop_step(i, carry):
        ring_step(i, 2)

        @pl.when(jnp.logical_not(mine))
        def _():
            for k in range(2):
                u_direct_in(2 * (i - 1) + k).wait_recv()
                u_mate(2 * (i - 1) + k).start()
        return carry

    lax.fori_loop(1, 5, loop_step, 0)
    ring_step(5, 2)

    @pl.when(jnp.logical_not(mine))
    def _():
        def wait_u(k, carry):
            u_mate_in(k).wait_recv()
            return carry

        lax.fori_loop(0, 8, wait_u, 0)

    @pl.when(mine)
    def _():
        u_local.wait()

    lax.fori_loop(0, 5, blocks, 0)
    ring_step(6, 2)
    lax.fori_loop(5, 10, blocks, 0)
    ring_step(7, 1)
    lax.fori_loop(10, 13, blocks, 0)
    for d in range(2):
        ring_in(d, d, 8).wait_recv()
        sib(15, (z + 8) % NZ, d).start()
    lax.fori_loop(13, 16, blocks, 0)

    mean_sq = jnp.sum(ssq[...].T, axis=0, keepdims=True) * (1.0 / 8192.0)
    r_row = lax.rsqrt(mean_sq + norm_eps)
    logits = acc[...] * r_row
    acc[...] = logits
    lg_copy = rcopy(acc, accb, lg_sem.at[0], lg_sem.at[1], sibling)
    lg_copy.start()

    def as_tile(row):
        return [row[:, 128 * k:128 * k + 128] for k in range(4)]

    def as_row(tile):
        return jnp.concatenate([tile[k:k + 1, :] for k in range(4)], axis=1)

    m = jnp.max(logits, axis=0, keepdims=True)
    ex = jnp.sum(jnp.exp(logits - m), axis=0, keepdims=True)
    zst[z] = jnp.concatenate(as_tile(m) + as_tile(ex), axis=0)

    def z_exchange(buf, ss, rr):
        def out(k):
            return rcopy(buf.at[z], buf.at[z], ss.at[k], rr.at[k], dev(x, y, (z + k) % NZ, c))

        def into(k):
            slot = (z + NZ - k) % NZ
            return rcopy(buf.at[slot], buf.at[slot], ss.at[k], rr.at[k], dev(x, y, (z + k) % NZ, c))

        def go(make, act):
            def body(k, carry):
                act(make(k))
                return carry

            lax.fori_loop(1, NZ, body, 0)

        return (lambda: go(out, lambda a: a.start()), lambda: go(into, lambda a: a.wait_recv()),
                lambda: go(out, lambda a: a.wait_send()))

    z_start, z_wait, z_done = z_exchange(zst, z_s, z_r)
    zt_start, zt_wait, zt_done = z_exchange(zt, zt_s, zt_r)
    z_start()

    t_copy.wait_recv()
    t2x = jnp.where(mine, tsrc[0:2, :], tbuf[0:2, :])
    tgt = jnp.concatenate([t2x[0:1, :], t2x[1:2, :], t2x[0:1, :], t2x[1:2, :]], axis=1)
    scale_row = jnp.where(lax.broadcasted_iota(jnp.int32, (1, 512), 1) < 256, scale_ref[0], scale_ref[1])
    rows_of = lax.broadcasted_iota(jnp.int32, (256, 512), 0)

    def is_target(plane):
        return (rows_of + (plane * NZ + z) * 256).astype(F32) == tgt

    def lane_sum(row):
        return row[:, :128] + row[:, 128:256] + row[:, 256:384] + row[:, 384:]

    t_part = lane_sum(jnp.sum(jnp.where(is_target(c), logits, 0.0), axis=0, keepdims=True) * scale_row)
    zt[z] = jnp.broadcast_to(t_part, (8, 128))

    z_wait()
    st = zst[...]
    m16, s16 = st[:, 0:4, :], st[:, 4:8, :]
    top = jnp.max(m16, axis=0)
    lebuf[c] = jnp.concatenate([top, jnp.sum(s16 * jnp.exp(m16 - top[None]), axis=0)], axis=0)
    le_copy = rcopy(lebuf.at[c], lebuf.at[c], le_sem.at[0], le_sem.at[1], sibling)
    le_in = rcopy(lebuf.at[1 - c], lebuf.at[1 - c], le_sem.at[0], le_sem.at[1], sibling)
    le_copy.start()
    zt_start()
    lg_copy.wait_recv()
    le_in.wait_recv()
    m_a, m_b = lebuf[0, 0:4, :], lebuf[1, 0:4, :]
    m_all = jnp.maximum(m_a, m_b)
    lse = m_all + jnp.log(lebuf[0, 4:8, :] * jnp.exp(m_a - m_all) + lebuf[1, 4:8, :] * jnp.exp(m_b - m_all))
    lse_row = as_row(lse)
    weight = scale_row * r_row
    gbuf[c] = (weight * (jnp.exp(acc[...] - lse_row) - is_target(c).astype(F32))).astype(BF16)
    gbuf[1 - c] = (weight * (jnp.exp(accb[...] - lse_row) - is_target(1 - c).astype(F32))).astype(BF16)

    def tp_exchange():
        zt_wait()
        tpair[c] = jnp.sum(zt[...], axis=0)
        tp_copy.start()

    tp_copy = rcopy(tpair.at[c], tpair.at[c], tp_sem.at[0], tp_sem.at[1], sibling)
    tp_in = rcopy(tpair.at[1 - c], tpair.at[1 - c], tp_sem.at[0], tp_sem.at[1], sibling)

    def l_copy(axis, k):
        if axis == 0:
            return rcopy(lx.at[x], lx.at[x], l_s.at[0, k], l_r.at[0, k], dev((x + k) % 4, y, z, c))
        return rcopy(ly.at[y], ly.at[y], l_s.at[1, k], l_r.at[1, k], dev(x, (y + k) % 4, z, c))

    def l_in(axis, k):
        if axis == 0:
            slot = (x + 4 - k) % 4
            return rcopy(lx.at[slot], lx.at[slot], l_s.at[0, k], l_r.at[0, k], dev((x + k) % 4, y, z, c))
        slot = (y + 4 - k) % 4
        return rcopy(ly.at[slot], ly.at[slot], l_s.at[1, k], l_r.at[1, k], dev(x, (y + k) % 4, z, c))

    def loss_x():
        tp_in.wait_recv()
        lx[x] = jnp.broadcast_to(lane_sum(scale_row * lse_row), (8, 128)) - (tpair[0] + tpair[1])
        for k in range(1, 4):
            l_copy(0, k).start()

    def loss_y():
        for k in range(1, 4):
            l_in(0, k).wait_recv()
        ly[y] = lx[0] + lx[1] + lx[2] + lx[3]
        for k in range(1, 4):
            l_copy(1, k).start()

    def loss_end():
        for k in range(1, 4):
            l_in(1, k).wait_recv()
        tot = ly[0] + ly[1] + ly[2] + ly[3]
        loss_ref[0] = jnp.sum(tot[0:1, :]) * (1.0 / 4096.0)

    def along(axis, step):
        if axis == 0:
            return dev((x + step) % 4, y, z, c)
        return dev(x, (y + step) % 4, z, c)

    def grad_block(dy, dx):
        y_, x_ = (y + dy) % 4, (x + dx) % 4
        s = ((y_ * 2 + x_ % 2) * 2 + c) * 2
        plane, slot = s // NZ, s % NZ
        for k in range(2):
            pbuf[y_, x_, :, 256 * k:256 * k + 256] = jnp.dot(
                gbuf[x_ // 2], abuf[plane, slot + k], preferred_element_type=F32).astype(BF16)

    def blk(axis, step, o):
        if axis == 0:
            return pbuf.at[(y + o) % 4, (x + step) % 4]
        return pbuf.at[(y + step) % 4, (x + o) % 4]

    def part(axis, which):
        return pl.ds(128 * axis + 64 * which, 64)

    STEP = (1, 3)

    def send_o(axis, d, o):
        return rcopy(blk(axis, 2, o).at[part(axis, d)], r_o.at[axis, d, o], rs_s.at[0, axis, d, o], rs_r.at[0, axis, d, o], along(axis, STEP[d]))

    def send_d(axis, d, o):
        return rcopy(blk(axis, STEP[d], o).at[part(axis, 1 - d)], r_d.at[axis, d, o], rs_s.at[1, axis, d, o], rs_r.at[1, axis, d, o], along(axis, STEP[d]))

    def send_c(axis, d, o):
        return rcopy(blk(axis, STEP[d], o).at[part(axis, d)], r_c.at[axis, d, o], rs_s.at[2, axis, d, o], rs_r.at[2, axis, d, o], along(axis, STEP[d]))

    def send_o2(axis, d):
        return rcopy(blk(axis, 0, 2).at[part(axis, d)], q_o.at[axis, d], qs_s.at[0, axis, d], qs_r.at[0, axis, d], along(1 - axis, STEP[d]))

    def send_d2(axis, d):
        return rcopy(blk(axis, 0, STEP[d]).at[part(axis, 1 - d)], q_d.at[axis, d], qs_s.at[1, axis, d], qs_r.at[1, axis, d], along(1 - axis, STEP[d]))

    def send_c2(axis, d):
        return rcopy(blk(axis, 0, STEP[d]).at[part(axis, d)], q_c.at[axis, d], qs_s.at[2, axis, d], qs_r.at[2, axis, d], along(1 - axis, STEP[d]))

    def start_o(axis, o):
        for d in range(2):
            send_o(axis, d, o).start()

    def start_d(axis, o):
        for d in range(2):
            send_d(axis, d, o).start()

    ORDER = (2, 1, 3, 0)
    grad_block(2, 2)
    start_o(0, 2)
    start_o(1, 2)

    def o_blocks(k, carry):
        o = k
        grad_block(o, 2)
        start_o(0, o)
        grad_block(2, o)
        start_o(1, o)
        return carry

    o_blocks(1, 0)
    o_blocks(3, 0)
    o_blocks(0, 0)
    start_d(0, 2)
    start_d(1, 2)
    for dy in (1, 3):
        for dx in (1, 3):
            grad_block(dy, dx)
    for o in (1, 3):
        start_d(0, o)
        start_d(1, o)
    for dd in (1, 3):
        grad_block(0, dd)
        grad_block(dd, 0)
    start_d(0, 0)
    start_d(1, 0)
    grad_block(0, 0)
    tp_exchange()

    for o in ORDER:
        for axis in range(2):
            for d in range(2):
                send_o(axis, d, o).wait_recv()
                ref = blk(axis, STEP[d], o)
                rows = part(axis, d)
                ref[rows, :] = (ref[rows, :].astype(F32) + r_o[axis, d, o].astype(F32)).astype(BF16)
                send_c(axis, d, o).start()
    loss_x()

    for o in ORDER:
        for axis in range(2):
            own = blk(axis, 0, o)
            for w in range(2):
                send_c(axis, w, o).wait_recv()
                send_d(axis, 1 - w, o).wait_recv()
                rows = part(axis, w)
                total = own[rows, :].astype(F32) + r_c[axis, w, o].astype(F32) + r_d[axis, 1 - w, o].astype(F32)
                if o == 0:
                    fin[rows, :] = total
                else:
                    own[rows, :] = total.astype(BF16)
            if o == 2:
                for d in range(2):
                    send_o2(axis, d).start()
            if o in STEP:
                send_d2(axis, STEP.index(o)).start()

    for axis in range(2):
        for d in range(2):
            send_o2(axis, d).wait_recv()
            ref = blk(axis, 0, STEP[d])
            rows = part(axis, d)
            ref[rows, :] = (ref[rows, :].astype(F32) + q_o[axis, d].astype(F32)).astype(BF16)
            send_c2(axis, d).start()

    loss_y()
    s_own = ((y * 2 + xl) * 2 + c) * 2
    gain_own = jnp.concatenate([gain_row(s_own), gain_row(s_own + 1)], axis=1)
    for axis in range(2):
        for w in range(2):
            send_c2(axis, w).wait_recv()
            send_d2(axis, 1 - w).wait_recv()
            rows = part(axis, w)
            fin[rows, :] = (fin[rows, :] + q_c[axis, w].astype(F32) + q_d[axis, 1 - w].astype(F32)) * gain_own
        o_ref[:, 128 * axis:128 * axis + 128] = fin[pl.ds(128 * axis, 128), :].T

    loss_end()

    for axis in range(2):
        for d in range(2):
            for o in range(4):
                send_o(axis, d, o).wait_send()
                send_d(axis, d, o).wait_send()
                send_c(axis, d, o).wait_send()
            send_o2(axis, d).wait_send()
            send_d2(axis, d).wait_send()
            send_c2(axis, d).wait_send()
    for axis in range(2):
        for k in range(1, 4):
            l_copy(axis, k).wait_send()
    for copy in (t_copy, lg_copy, le_copy, tp_copy):
        copy.wait_send()

    z_done()
    zt_done()

    def ring_done(i, carry):
        for h in range(2):
            for d in range(2):
                ring(d, h, i).wait_send()
        return carry

    lax.fori_loop(1, 8, ring_done, 0)
    for d in range(2):
        ring(d, d, 8).wait_send()

    def sib_done(n, carry):
        for h in range(2):
            sib(n, block_slot(n), h).wait_send()
        return carry

    lax.fori_loop(0, 16, sib_done, 0)

    @pl.when(mine)
    def _():
        def done(k, carry):
            u_direct(k).wait_send()
            return carry

        lax.fori_loop(0, 8, done, 0)

    @pl.when(jnp.logical_not(mine))
    def _():
        swap.wait_send()

        def done(k, carry):
            u_mate(k).wait_send()
            return carry

        lax.fori_loop(0, 8, done, 0)


def per_device(hidden_states, exit_layers, targets, norm_gain, exit_scale, unembedding):
    vmem = pl.BlockSpec(memory_space=pltpu.VMEM)
    smem = pl.BlockSpec(memory_space=pltpu.SMEM)
    anywhere = pl.BlockSpec(memory_space=pl.ANY)
    dma = pltpu.SemaphoreType.DMA
    grad, loss = pl.pallas_call(
        kernel,
        out_shape=(jax.ShapeDtypeStruct((512, 256), F32), jax.ShapeDtypeStruct((1,), F32)),
        in_specs=[anywhere] * 6,
        out_specs=(vmem, smem),
        scratch_shapes=[
            pltpu.SMEM((2, 4), jnp.int32), pltpu.SMEM((2,), F32), pltpu.VMEM((2, 128), jnp.int32),
            pltpu.VMEM((64, 128), BF16),
            pltpu.VMEM((4, 256, 256), BF16),
            pltpu.VMEM((512, 256), BF16),
            pltpu.VMEM((8, 128), F32),
            pltpu.VMEM((64, 128), F32),
            dma((5,)),
            pltpu.VMEM((2, 16, 512, 256), BF16),
            pltpu.VMEM((32, 256, 256), BF16),
            pltpu.VMEM((256, 512), F32),
            pltpu.VMEM((256, 512), F32),
            pltpu.VMEM((512, 128), F32),
            pltpu.VMEM((2, 256, 512), BF16),
            pltpu.VMEM((8, 128), F32),
            pltpu.VMEM((16, 8, 128), F32),
            pltpu.VMEM((16, 8, 128), F32),
            pltpu.VMEM((2, 8, 128), F32),
            pltpu.VMEM((2, 8, 128), F32),
            pltpu.VMEM((4, 8, 128), F32),
            pltpu.VMEM((4, 8, 128), F32),
            pltpu.VMEM((4, 4, 256, 512), BF16),
            pltpu.VMEM((256, 512), F32),
            pltpu.VMEM((2, 2, 4, 64, 512), BF16),
            pltpu.VMEM((2, 2, 4, 64, 512), BF16),
            pltpu.VMEM((2, 2, 4, 64, 512), BF16),
            pltpu.VMEM((2, 2, 64, 512), BF16),
            pltpu.VMEM((2, 2, 64, 512), BF16),
            pltpu.VMEM((2, 2, 64, 512), BF16),
            dma((2,)), dma((2, 2, 8)), dma((2, 2, 8)), dma((16, 2)), dma((16, 2)),
            dma((2, 8)), dma((2, 8)), dma, dma((2,)), dma((2,)), dma((16,)), dma((16,)), dma((16,)), dma((16,)), dma((2,)),
            dma((2,)), dma((2, 4)), dma((2, 4)), dma((3, 2, 2, 4)), dma((3, 2, 2, 4)), dma((3, 2, 2)), dma((3, 2, 2)),
        ],
        compiler_params=pltpu.CompilerParams(
            collective_id=0, has_side_effects=True, vmem_limit_bytes=56 << 20),
    )(exit_layers.T, exit_scale, hidden_states, unembedding.reshape(32, 256, 256),
      targets.reshape(2, 128), norm_gain.reshape(64, 128))
    return (grad, loss.reshape(()))


def solution(mesh):
    in_specs = (P(None, "dp", "vocab"), P("dp", None), P("dp"), P(), P(), P(None, "vocab"))
    out_specs = (P("dp", "vocab"), P())
    return jax.shard_map(
        per_device, mesh=mesh, in_specs=in_specs, out_specs=out_specs, check_vma=False
    )
```

```python
import jax
import jax.numpy as jnp
from jax import lax
from jax.experimental import pallas as pl
from jax.experimental.pallas import tpu as pltpu
from jax.sharding import PartitionSpec as P

norm_eps = 1e-05
MESH = pl.DeviceIdType.MESH
F32 = jnp.float32
BF16 = jnp.bfloat16
NZ, NX, NY = 16, 4, 4


def kernel(el_any, scale_any, hid_ref, u_ref, tgt_any, gain_any, o_ref, loss_ref,
           el_ref, scale_ref, tgt_ref, gain_ref, hbuf, xbuf, tsrc, gain, in_sem,
           abuf, ubuf, acc, accb, ssq, gbuf, tbuf, zst, zt, lebuf, tpair, lx, ly, pbuf, fin,
           r_o, r_d, r_c, q_o, q_d, q_c,
           swap_sem, ring_s, ring_r, sib_s, sib_r, u_s, u_r, u_loc, t_sem, lg_sem, z_s, z_r, zt_s, zt_r, le_sem,
           tp_sem, l_s, l_r, rs_s, rs_r, qs_s, qs_r):
    dp = lax.axis_index("dp")
    vo = lax.axis_index("vocab")
    c = dp % 2
    xl = (dp // 2) % 2
    y = dp // 4
    z = vo % NZ
    xh = vo // NZ
    x = xh * 2 + xl

    def dev(x_, y_, z_, c_):
        return ((y_ * 2 + x_ % 2) * 2 + c_, (x_ // 2) * NZ + z_)

    sibling = dev(x, y, z, 1 - c)
    partner = dev((x + 2) % 4, y, z, 1 - c)

    def rcopy(src, dst, s, r, to):
        return pltpu.make_async_remote_copy(src_ref=src, dst_ref=dst, send_sem=s, recv_sem=r,
                                            device_id=to, device_id_type=MESH)

    bar = pltpu.get_barrier_semaphore()
    for to in (sibling, partner, dev(x, y, (z + 1) % NZ, c), dev(x, y, (z + NZ - 1) % NZ, c)):
        pl.semaphore_signal(bar, inc=1, device_id=to, device_id_type=MESH)
    for k in range(1, 4):
        pl.semaphore_signal(bar, inc=1, device_id=dev((x + k) % 4, y, z, c), device_id_type=MESH)
        pl.semaphore_signal(bar, inc=1, device_id=dev(x, (y + k) % 4, z, c), device_id_type=MESH)

    inputs = [pltpu.make_async_copy(a, b, in_sem.at[k]) for k, (a, b) in enumerate((
        (hid_ref, hbuf), (el_any, el_ref), (scale_any, scale_ref), (tgt_any, tgt_ref), (gain_any, gain_ref)))]
    for copy in inputs:
        copy.start()

    def select(dst):
        for e in range(2):
            for row in range(4):
                dst[pl.ds(256 * e + 64 * row, 64), :] = hbuf[el_ref[e, row], pl.ds(64 * row, 64), :]

    mine = c == xh
    for copy in inputs:
        copy.wait()

    @pl.when(mine)
    def _():
        select(abuf.at[c, z])

    @pl.when(jnp.logical_not(mine))
    def _():
        select(xbuf)

    pl.semaphore_wait(bar, 10)

    def swap(h):
        rows = pl.ds(256 * h, 256)
        return rcopy(xbuf.at[rows], abuf.at[1 - c, z, rows], swap_sem.at[0, h], swap_sem.at[1, h], partner)

    def swap_in(h):
        ref = abuf.at[c, z, pl.ds(256 * h, 256)]
        return rcopy(ref, ref, swap_sem.at[0, h], swap_sem.at[1, h], partner)

    def u_direct(k):
        j = (1 - xl) * 8 + k
        return rcopy(u_ref.at[pl.ds(2 * j, 2)], ubuf.at[pl.ds(2 * j, 2)], u_s.at[0, k], u_r.at[0, k], dev(3 - x, y, z, c))

    def u_direct_in(k):
        j = xl * 8 + k
        return rcopy(ubuf.at[pl.ds(2 * j, 2)], ubuf.at[pl.ds(2 * j, 2)], u_s.at[0, k], u_r.at[0, k], dev(3 - x, y, z, c))

    def u_mate(k):
        j = xl * 8 + k
        return rcopy(ubuf.at[pl.ds(2 * j, 2)], ubuf.at[pl.ds(2 * j, 2)], u_s.at[1, k], u_r.at[1, k], dev(xh * 2 + 1 - xl, y, z, c))

    def u_mate_in(k):
        j = (1 - xl) * 8 + k
        return rcopy(ubuf.at[pl.ds(2 * j, 2)], ubuf.at[pl.ds(2 * j, 2)], u_s.at[1, k], u_r.at[1, k], dev(xh * 2 + 1 - xl, y, z, c))

    u_local = pltpu.make_async_copy(u_ref, ubuf, u_loc)

    @pl.when(jnp.logical_not(mine))
    def _():
        for h in range(2):
            swap(h).start()

    tsrc[0:2, :] = tgt_ref[...].astype(F32)
    t_copy = rcopy(tsrc, tbuf, t_sem.at[0], t_sem.at[1], sibling)
    t_copy.start()

    @pl.when(mine)
    def _():
        u_local.start()

        def send_u(k, carry):
            u_direct(k).start()
            return carry

        lax.fori_loop(0, 8, send_u, 0)

    def step_slot(d, i):
        return (z - i + NZ) % NZ if d == 0 else (z + i) % NZ

    def half(slot, h):
        return abuf.at[c, slot, pl.ds(256 * h, 256)]

    def ring(d, h, i):
        ref = half(step_slot(d, i - 1), h)
        to = dev(x, y, (z + 1) % NZ, c) if d == 0 else dev(x, y, (z + NZ - 1) % NZ, c)
        return rcopy(ref, ref, ring_s.at[d, h, i - 1], ring_r.at[d, h, i - 1], to)

    def ring_in(d, h, i):
        ref = half(step_slot(d, i), h)
        to = dev(x, y, (z + 1) % NZ, c) if d == 0 else dev(x, y, (z + NZ - 1) % NZ, c)
        return rcopy(ref, ref, ring_s.at[d, h, i - 1], ring_r.at[d, h, i - 1], to)

    def sib(n, slot, h):
        ref = half(slot, h)
        return rcopy(ref, ref, sib_s.at[n, h], sib_r.at[n, h], sibling)

    def sib_in(n, slot, h):
        ref = abuf.at[1 - c, slot, pl.ds(256 * h, 256)]
        return rcopy(ref, ref, sib_s.at[n, h], sib_r.at[n, h], sibling)

    for h in range(2):
        @pl.when(jnp.logical_not(mine))
        def _():
            swap_in(h).wait_recv()

        for d in range(2):
            ring(d, h, 1).start()
    for h in range(2):
        sib(0, z, h).start()

    gain[...] = gain_ref[...].astype(F32)

    def gain_row(s):
        return jnp.concatenate([gain[pl.ds(2 * s, 1), :], gain[pl.ds(2 * s + 1, 1), :]], axis=1)

    acc[0:256, :] = jnp.zeros((256, 512), F32)
    ssq[...] = jnp.zeros_like(ssq)

    def ring_step(i, more):
        for h in range(2):
            for d in range(2):
                ring_in(d, h, i).wait_recv()
                if more == 2 or (more == 1 and h == d):
                    ring(d, h, i + 1).start()
                sib(2 * i - d, step_slot(d, i), h).start()

    def block_slot(n):
        off = jnp.where(n % 2 == 1, (n + 1) // 2, NZ - n // 2)
        return (z + off) % NZ

    def blocks(n, carry):
        slot = block_slot(n)
        for h in range(2):
            sib_in(n, slot, h).wait_recv()
        for cs in range(2):
            s = cs * NZ + slot
            a = abuf[cs, slot].astype(F32)
            ssq[...] += a[:, :128] * a[:, :128] + a[:, 128:] * a[:, 128:]
            ag = (a * gain_row(s)).astype(BF16)
            acc[0:256, :] += lax.dot_general(ubuf[s], ag, (((0,), (1,)), ((), ())), preferred_element_type=F32)
        return carry

    def loop_step(i, carry):
        ring_step(i, 2)

        @pl.when(jnp.logical_not(mine))
        def _():
            for k in range(2):
                u_direct_in(2 * (i - 1) + k).wait_recv()
                u_mate(2 * (i - 1) + k).start()
        return carry

    lax.fori_loop(1, 5, loop_step, 0)
    ring_step(5, 2)

    @pl.when(jnp.logical_not(mine))
    def _():
        def wait_u(k, carry):
            u_mate_in(k).wait_recv()
            return carry

        lax.fori_loop(0, 8, wait_u, 0)

    @pl.when(mine)
    def _():
        u_local.wait()

    lax.fori_loop(0, 5, blocks, 0)
    ring_step(6, 2)
    lax.fori_loop(5, 10, blocks, 0)
    ring_step(7, 1)
    lax.fori_loop(10, 15, blocks, 0)
    for d in range(2):
        ring_in(d, d, 8).wait_recv()
        sib(15, (z + 8) % NZ, d).start()
    blocks(15, 0)

    mean_sq = jnp.sum(ssq[...].T, axis=0, keepdims=True) * (1.0 / 8192.0)
    r_row = lax.rsqrt(mean_sq + norm_eps)
    logits = acc[0:256, :] * r_row
    def as_tile(row):
        return [row[:, 128 * k:128 * k + 128] for k in range(4)]

    def as_row(tile):
        return jnp.concatenate([tile[k:k + 1, :] for k in range(4)], axis=1)

    m = jnp.max(logits, axis=0, keepdims=True)
    ex = jnp.exp(logits - m)
    acc[0:256, :] = ex
    acc[256:264, :] = jnp.broadcast_to(m, (8, 512))
    zst[z] = jnp.concatenate(as_tile(m) + as_tile(jnp.sum(ex, axis=0, keepdims=True)), axis=0)

    def z_exchange(buf, ss, rr):
        def out(k):
            return rcopy(buf.at[z], buf.at[z], ss.at[k], rr.at[k], dev(x, y, (z + k) % NZ, c))

        def into(k):
            slot = (z + NZ - k) % NZ
            return rcopy(buf.at[slot], buf.at[slot], ss.at[k], rr.at[k], dev(x, y, (z + k) % NZ, c))

        def go(make, act):
            def body(k, carry):
                act(make(k))
                return carry

            lax.fori_loop(1, NZ, body, 0)

        return (lambda: go(out, lambda a: a.start()), lambda: go(into, lambda a: a.wait_recv()),
                lambda: go(out, lambda a: a.wait_send()))

    z_start, z_wait, z_done = z_exchange(zst, z_s, z_r)
    zt_start, zt_wait, zt_done = z_exchange(zt, zt_s, zt_r)
    z_start()
    lg_copy = rcopy(acc, accb, lg_sem.at[0], lg_sem.at[1], sibling)
    lg_copy.start()

    t_copy.wait_recv()
    t2x = jnp.where(mine, tsrc[0:2, :], tbuf[0:2, :])
    tgt = jnp.concatenate([t2x[0:1, :], t2x[1:2, :], t2x[0:1, :], t2x[1:2, :]], axis=1)
    scale_row = jnp.where(lax.broadcasted_iota(jnp.int32, (1, 512), 1) < 256, scale_ref[0], scale_ref[1])
    rows_of = lax.broadcasted_iota(jnp.int32, (256, 512), 0)

    def is_target(plane):
        return (rows_of + (plane * NZ + z) * 256).astype(F32) == tgt

    def lane_sum(row):
        return row[:, :128] + row[:, 128:256] + row[:, 256:384] + row[:, 384:]

    t_part = lane_sum(jnp.sum(jnp.where(is_target(c), logits, 0.0), axis=0, keepdims=True) * scale_row)
    zt[z] = jnp.broadcast_to(t_part, (8, 128))

    z_wait()
    st = zst[...]
    m16, s16 = st[:, 0:4, :], st[:, 4:8, :]
    top = jnp.max(m16, axis=0)
    lebuf[c] = jnp.concatenate([top, jnp.sum(s16 * jnp.exp(m16 - top[None]), axis=0)], axis=0)
    le_copy = rcopy(lebuf.at[c], lebuf.at[c], le_sem.at[0], le_sem.at[1], sibling)
    le_in = rcopy(lebuf.at[1 - c], lebuf.at[1 - c], le_sem.at[0], le_sem.at[1], sibling)
    le_copy.start()
    lg_copy.wait_recv()
    le_in.wait_recv()
    m_a, m_b = lebuf[0, 0:4, :], lebuf[1, 0:4, :]
    m_all = jnp.maximum(m_a, m_b)
    lse = m_all + jnp.log(lebuf[0, 4:8, :] * jnp.exp(m_a - m_all) + lebuf[1, 4:8, :] * jnp.exp(m_b - m_all))
    lse_row = as_row(lse)
    weight = scale_row * r_row

    def gradient(plane, buf):
        share = jnp.exp(buf[256:257, :] - lse_row)
        gbuf[plane] = (weight * (buf[0:256, :] * share - is_target(plane).astype(F32))).astype(BF16)

    gradient(c, acc)
    gradient(1 - c, accb)

    def tp_exchange():
        zt_wait()
        tpair[c] = jnp.sum(zt[...], axis=0)
        tp_copy.start()

    tp_copy = rcopy(tpair.at[c], tpair.at[c], tp_sem.at[0], tp_sem.at[1], sibling)
    tp_in = rcopy(tpair.at[1 - c], tpair.at[1 - c], tp_sem.at[0], tp_sem.at[1], sibling)

    def l_copy(axis, k):
        if axis == 0:
            return rcopy(lx.at[x], lx.at[x], l_s.at[0, k], l_r.at[0, k], dev((x + k) % 4, y, z, c))
        return rcopy(ly.at[y], ly.at[y], l_s.at[1, k], l_r.at[1, k], dev(x, (y + k) % 4, z, c))

    def l_in(axis, k):
        if axis == 0:
            slot = (x + 4 - k) % 4
            return rcopy(lx.at[slot], lx.at[slot], l_s.at[0, k], l_r.at[0, k], dev((x + k) % 4, y, z, c))
        slot = (y + 4 - k) % 4
        return rcopy(ly.at[slot], ly.at[slot], l_s.at[1, k], l_r.at[1, k], dev(x, (y + k) % 4, z, c))

    def loss_x():
        tp_in.wait_recv()
        lx[x] = jnp.broadcast_to(lane_sum(scale_row * lse_row), (8, 128)) - (tpair[0] + tpair[1])
        for k in range(1, 4):
            l_copy(0, k).start()

    def loss_y():
        for k in range(1, 4):
            l_in(0, k).wait_recv()
        ly[y] = lx[0] + lx[1] + lx[2] + lx[3]
        for k in range(1, 4):
            l_copy(1, k).start()

    def loss_end():
        for k in range(1, 4):
            l_in(1, k).wait_recv()
        tot = ly[0] + ly[1] + ly[2] + ly[3]
        loss_ref[0] = jnp.sum(tot[0:1, :]) * (1.0 / 4096.0)

    def along(axis, step):
        if axis == 0:
            return dev((x + step) % 4, y, z, c)
        return dev(x, (y + step) % 4, z, c)

    def grad_block(dy, dx):
        y_, x_ = (y + dy) % 4, (x + dx) % 4
        s = ((y_ * 2 + x_ % 2) * 2 + c) * 2
        plane, slot = s // NZ, s % NZ
        for k in range(2):
            pbuf[y_, x_, :, 256 * k:256 * k + 256] = jnp.dot(
                gbuf[x_ // 2], abuf[plane, slot + k], preferred_element_type=F32).astype(BF16)

    def blk(axis, step, o):
        if axis == 0:
            return pbuf.at[(y + o) % 4, (x + step) % 4]
        return pbuf.at[(y + step) % 4, (x + o) % 4]

    def part(axis, which):
        return pl.ds(128 * axis + 64 * which, 64)

    STEP = (1, 3)

    def send_o(axis, d, o):
        return rcopy(blk(axis, 2, o).at[part(axis, d)], r_o.at[axis, d, o], rs_s.at[0, axis, d, o], rs_r.at[0, axis, d, o], along(axis, STEP[d]))

    def send_d(axis, d, o):
        return rcopy(blk(axis, STEP[d], o).at[part(axis, 1 - d)], r_d.at[axis, d, o], rs_s.at[1, axis, d, o], rs_r.at[1, axis, d, o], along(axis, STEP[d]))

    def send_c(axis, d, o):
        return rcopy(blk(axis, STEP[d], o).at[part(axis, d)], r_c.at[axis, d, o], rs_s.at[2, axis, d, o], rs_r.at[2, axis, d, o], along(axis, STEP[d]))

    def send_o2(axis, d):
        return rcopy(blk(axis, 0, 2).at[part(axis, d)], q_o.at[axis, d], qs_s.at[0, axis, d], qs_r.at[0, axis, d], along(1 - axis, STEP[d]))

    def send_d2(axis, d):
        return rcopy(blk(axis, 0, STEP[d]).at[part(axis, 1 - d)], q_d.at[axis, d], qs_s.at[1, axis, d], qs_r.at[1, axis, d], along(1 - axis, STEP[d]))

    def send_c2(axis, d):
        return rcopy(blk(axis, 0, STEP[d]).at[part(axis, d)], q_c.at[axis, d], qs_s.at[2, axis, d], qs_r.at[2, axis, d], along(1 - axis, STEP[d]))

    def start_o(axis, o):
        for d in range(2):
            send_o(axis, d, o).start()

    def start_d(axis, o):
        for d in range(2):
            send_d(axis, d, o).start()

    def pair_sum(axis, d, o):
        send_o(axis, d, o).wait_recv()
        ref = blk(axis, STEP[d], o)
        rows = part(axis, d)
        ref[rows, :] = ref[rows, :] + r_o[axis, d, o]
        send_c(axis, d, o).start()

    def pair_sums(o):
        for axis in range(2):
            for d in range(2):
                pair_sum(axis, d, o)

    def first_pass(o):
        for axis in range(2):
            own = blk(axis, 0, o)
            for w in range(2):
                send_c(axis, w, o).wait_recv()
                send_d(axis, 1 - w, o).wait_recv()
                rows = part(axis, w)
                total = own[rows, :].astype(F32) + r_c[axis, w, o].astype(F32) + r_d[axis, 1 - w, o].astype(F32)
                if o == 0:
                    fin[rows, :] = total
                else:
                    own[rows, :] = total.astype(BF16)
                if o == 2:
                    send_o2(axis, w).start()
            if o in STEP:
                send_d2(axis, STEP.index(o)).start()

    def both(start, o):
        for axis in range(2):
            start(axis, o)

    grad_block(2, 2)
    both(start_o, 2)
    for o in (1, 3, 0):
        grad_block(o, 2)
        start_o(0, o)
        grad_block(2, o)
        start_o(1, o)
    both(start_d, 2)
    zt_start()
    pair_sums(2)
    for dy in (1, 3):
        for dx in (1, 3):
            grad_block(dy, dx)
    both(start_d, 1)
    both(start_d, 3)
    pair_sums(1)
    pair_sums(3)
    tp_exchange()
    first_pass(2)
    for k in (1, 3):
        grad_block(0, k)
        grad_block(k, 0)
    both(start_d, 0)
    pair_sums(0)
    loss_x()
    first_pass(1)
    first_pass(3)
    loss_y()
    grad_block(0, 0)
    for axis in range(2):
        for d in range(2):
            send_o2(axis, d).wait_recv()
            ref = blk(axis, 0, STEP[d])
            rows = part(axis, d)
            ref[rows, :] = ref[rows, :] + q_o[axis, d]
            send_c2(axis, d).start()
    first_pass(0)
    s_own = ((y * 2 + xl) * 2 + c) * 2
    gain_own = jnp.concatenate([gain_row(s_own), gain_row(s_own + 1)], axis=1)
    for axis in range(2):
        for w in range(2):
            send_c2(axis, w).wait_recv()
            send_d2(axis, 1 - w).wait_recv()
            rows = part(axis, w)
            fin[rows, :] = (fin[rows, :] + q_c[axis, w].astype(F32) + q_d[axis, 1 - w].astype(F32)) * gain_own
        o_ref[:, 128 * axis:128 * axis + 128] = fin[pl.ds(128 * axis, 128), :].T

    loss_end()

    for axis in range(2):
        for d in range(2):
            for o in range(4):
                send_o(axis, d, o).wait_send()
                send_d(axis, d, o).wait_send()
                send_c(axis, d, o).wait_send()
            send_o2(axis, d).wait_send()
            send_d2(axis, d).wait_send()
            send_c2(axis, d).wait_send()
    for axis in range(2):
        for k in range(1, 4):
            l_copy(axis, k).wait_send()
    for copy in (t_copy, lg_copy, le_copy, tp_copy):
        copy.wait_send()

    z_done()
    zt_done()

    def ring_done(i, carry):
        for h in range(2):
            for d in range(2):
                ring(d, h, i).wait_send()
        return carry

    lax.fori_loop(1, 8, ring_done, 0)
    for d in range(2):
        ring(d, d, 8).wait_send()

    def sib_done(n, carry):
        for h in range(2):
            sib(n, block_slot(n), h).wait_send()
        return carry

    lax.fori_loop(0, 16, sib_done, 0)

    @pl.when(mine)
    def _():
        def done(k, carry):
            u_direct(k).wait_send()
            return carry

        lax.fori_loop(0, 8, done, 0)

    @pl.when(jnp.logical_not(mine))
    def _():
        for h in range(2):
            swap(h).wait_send()

        def done(k, carry):
            u_mate(k).wait_send()
            return carry

        lax.fori_loop(0, 8, done, 0)


def per_device(hidden_states, exit_layers, targets, norm_gain, exit_scale, unembedding):
    vmem = pl.BlockSpec(memory_space=pltpu.VMEM)
    smem = pl.BlockSpec(memory_space=pltpu.SMEM)
    anywhere = pl.BlockSpec(memory_space=pltpu.HBM)
    dma = pltpu.SemaphoreType.DMA
    grad, loss = pl.pallas_call(
        kernel,
        out_shape=(jax.ShapeDtypeStruct((512, 256), F32), jax.ShapeDtypeStruct((1,), F32)),
        in_specs=[anywhere] * 6,
        out_specs=(vmem, smem),
        scratch_shapes=[
            pltpu.SMEM((2, 4), jnp.int32), pltpu.SMEM((2,), F32), pltpu.VMEM((2, 128), jnp.int32),
            pltpu.VMEM((64, 128), BF16),
            pltpu.VMEM((4, 256, 256), BF16),
            pltpu.VMEM((512, 256), BF16),
            pltpu.VMEM((8, 128), F32),
            pltpu.VMEM((64, 128), F32),
            dma((5,)),
            pltpu.VMEM((2, 16, 512, 256), BF16),
            pltpu.VMEM((32, 256, 256), BF16),
            pltpu.VMEM((264, 512), F32),
            pltpu.VMEM((264, 512), F32),
            pltpu.VMEM((512, 128), F32),
            pltpu.VMEM((2, 256, 512), BF16),
            pltpu.VMEM((8, 128), F32),
            pltpu.VMEM((16, 8, 128), F32),
            pltpu.VMEM((16, 8, 128), F32),
            pltpu.VMEM((2, 8, 128), F32),
            pltpu.VMEM((2, 8, 128), F32),
            pltpu.VMEM((4, 8, 128), F32),
            pltpu.VMEM((4, 8, 128), F32),
            pltpu.VMEM((4, 4, 256, 512), BF16),
            pltpu.VMEM((256, 512), F32),
            pltpu.VMEM((2, 2, 4, 64, 512), BF16),
            pltpu.VMEM((2, 2, 4, 64, 512), BF16),
            pltpu.VMEM((2, 2, 4, 64, 512), BF16),
            pltpu.VMEM((2, 2, 64, 512), BF16),
            pltpu.VMEM((2, 2, 64, 512), BF16),
            pltpu.VMEM((2, 2, 64, 512), BF16),
            dma((2, 2)), dma((2, 2, 8)), dma((2, 2, 8)), dma((16, 2)), dma((16, 2)),
            dma((2, 8)), dma((2, 8)), dma, dma((2,)), dma((2,)), dma((16,)), dma((16,)), dma((16,)), dma((16,)), dma((2,)),
            dma((2,)), dma((2, 4)), dma((2, 4)), dma((3, 2, 2, 4)), dma((3, 2, 2, 4)), dma((3, 2, 2)), dma((3, 2, 2)),
        ],
        compiler_params=pltpu.CompilerParams(
            collective_id=0, has_side_effects=True, vmem_limit_bytes=30 << 20),
    )(*[pltpu.with_memory_space_constraint(a, pltpu.HBM) for a in (
        exit_layers.T, exit_scale, hidden_states, unembedding.reshape(32, 256, 256),
        targets.reshape(2, 128), norm_gain.reshape(64, 128))])
    return (grad, loss.reshape(()))


def solution(mesh):
    in_specs = (P(None, "dp", "vocab"), P("dp", None), P("dp"), P(), P(), P(None, "vocab"))
    out_specs = (P("dp", "vocab"), P())
    return jax.shard_map(
        per_device, mesh=mesh, in_specs=in_specs, out_specs=out_specs, check_vma=False
    )
```

```python
import jax
import jax.numpy as jnp
from jax import lax
from jax.experimental import pallas as pl
from jax.experimental.pallas import tpu as pltpu
from jax.sharding import PartitionSpec as P

norm_eps = 1e-05
MESH = pl.DeviceIdType.MESH
F32 = jnp.float32
BF16 = jnp.bfloat16
NZ, NX, NY = 16, 4, 4


def kernel(el_any, scale_any, hid_ref, u_ref, tgt_any, gain_any, o_ref, loss_ref,
           el_ref, scale_ref, tgt_ref, gain_ref, hbuf, xbuf, tsrc, gain, in_sem,
           abuf, ubuf, acc, accb, ssq, gbuf, tbuf, zst, lebuf, lx, ly, pbuf, fin,
           r_o, r_d, r_c, q_o, q_d, q_c,
           swap_sem, ring_s, ring_r, sib_s, sib_r, u_s, u_r, u_loc, t_sem, lg_sem, z_s, z_r, le_sem,
           l_s, l_r, rs_s, rs_r, qs_s, qs_r):
    dp = lax.axis_index("dp")
    vo = lax.axis_index("vocab")
    c = dp % 2
    xl = (dp // 2) % 2
    y = dp // 4
    z = vo % NZ
    xh = vo // NZ
    x = xh * 2 + xl

    def dev(x_, y_, z_, c_):
        return ((y_ * 2 + x_ % 2) * 2 + c_, (x_ // 2) * NZ + z_)

    sibling = dev(x, y, z, 1 - c)
    partner = dev((x + 2) % 4, y, z, 1 - c)

    def rcopy(src, dst, s, r, to):
        return pltpu.make_async_remote_copy(src_ref=src, dst_ref=dst, send_sem=s, recv_sem=r,
                                            device_id=to, device_id_type=MESH)

    bar = pltpu.get_barrier_semaphore()
    for to in (sibling, partner, dev(x, y, (z + 1) % NZ, c), dev(x, y, (z + NZ - 1) % NZ, c)):
        pl.semaphore_signal(bar, inc=1, device_id=to, device_id_type=MESH)
    for k in range(1, 4):
        pl.semaphore_signal(bar, inc=1, device_id=dev((x + k) % 4, y, z, c), device_id_type=MESH)
        pl.semaphore_signal(bar, inc=1, device_id=dev(x, (y + k) % 4, z, c), device_id_type=MESH)

    inputs = [pltpu.make_async_copy(a, b, in_sem.at[k]) for k, (a, b) in enumerate((
        (hid_ref, hbuf), (el_any, el_ref), (scale_any, scale_ref), (tgt_any, tgt_ref), (gain_any, gain_ref)))]
    for copy in inputs:
        copy.start()

    def select(dst):
        for e in range(2):
            for row in range(4):
                dst[pl.ds(256 * e + 64 * row, 64), :] = hbuf[el_ref[e, row], pl.ds(64 * row, 64), :]

    mine = c == xh
    for copy in inputs:
        copy.wait()

    @pl.when(mine)
    def _():
        select(abuf.at[c, z])

    @pl.when(jnp.logical_not(mine))
    def _():
        select(xbuf)

    pl.semaphore_wait(bar, 10)

    def swap(h):
        rows = pl.ds(256 * h, 256)
        return rcopy(xbuf.at[rows], abuf.at[1 - c, z, rows], swap_sem.at[0, h], swap_sem.at[1, h], partner)

    def swap_in(h):
        ref = abuf.at[c, z, pl.ds(256 * h, 256)]
        return rcopy(ref, ref, swap_sem.at[0, h], swap_sem.at[1, h], partner)

    def u_direct(k):
        j = (1 - xl) * 8 + k
        return rcopy(u_ref.at[pl.ds(2 * j, 2)], ubuf.at[pl.ds(2 * j, 2)], u_s.at[0, k], u_r.at[0, k], dev(3 - x, y, z, c))

    def u_direct_in(k):
        j = xl * 8 + k
        return rcopy(ubuf.at[pl.ds(2 * j, 2)], ubuf.at[pl.ds(2 * j, 2)], u_s.at[0, k], u_r.at[0, k], dev(3 - x, y, z, c))

    def u_mate(k):
        j = xl * 8 + k
        return rcopy(ubuf.at[pl.ds(2 * j, 2)], ubuf.at[pl.ds(2 * j, 2)], u_s.at[1, k], u_r.at[1, k], dev(xh * 2 + 1 - xl, y, z, c))

    def u_mate_in(k):
        j = (1 - xl) * 8 + k
        return rcopy(ubuf.at[pl.ds(2 * j, 2)], ubuf.at[pl.ds(2 * j, 2)], u_s.at[1, k], u_r.at[1, k], dev(xh * 2 + 1 - xl, y, z, c))

    u_local = pltpu.make_async_copy(u_ref, ubuf, u_loc)

    @pl.when(jnp.logical_not(mine))
    def _():
        for h in range(2):
            swap(h).start()

    tsrc[0:2, :] = tgt_ref[...].astype(F32)
    t_copy = rcopy(tsrc, tbuf, t_sem.at[0], t_sem.at[1], sibling)
    t_copy.start()

    @pl.when(mine)
    def _():
        u_local.start()

        def send_u(k, carry):
            u_direct(k).start()
            return carry

        lax.fori_loop(0, 8, send_u, 0)

    def step_slot(d, i):
        return (z - i + NZ) % NZ if d == 0 else (z + i) % NZ

    def half(slot, h):
        return abuf.at[c, slot, pl.ds(256 * h, 256)]

    def ring(d, h, i):
        ref = half(step_slot(d, i - 1), h)
        to = dev(x, y, (z + 1) % NZ, c) if d == 0 else dev(x, y, (z + NZ - 1) % NZ, c)
        return rcopy(ref, ref, ring_s.at[d, h, i - 1], ring_r.at[d, h, i - 1], to)

    def ring_in(d, h, i):
        ref = half(step_slot(d, i), h)
        to = dev(x, y, (z + 1) % NZ, c) if d == 0 else dev(x, y, (z + NZ - 1) % NZ, c)
        return rcopy(ref, ref, ring_s.at[d, h, i - 1], ring_r.at[d, h, i - 1], to)

    def sib(n, slot, h):
        ref = half(slot, h)
        return rcopy(ref, ref, sib_s.at[n, h], sib_r.at[n, h], sibling)

    def sib_in(n, slot, h):
        ref = abuf.at[1 - c, slot, pl.ds(256 * h, 256)]
        return rcopy(ref, ref, sib_s.at[n, h], sib_r.at[n, h], sibling)

    for h in range(2):
        @pl.when(jnp.logical_not(mine))
        def _():
            swap_in(h).wait_recv()

        for d in range(2):
            ring(d, h, 1).start()
    for h in range(2):
        sib(0, z, h).start()

    gain[...] = gain_ref[...].astype(F32)

    def gain_row(s):
        return jnp.concatenate([gain[pl.ds(2 * s, 1), :], gain[pl.ds(2 * s + 1, 1), :]], axis=1)

    acc[0:256, :] = jnp.zeros((256, 512), F32)
    ssq[...] = jnp.zeros_like(ssq)

    def ring_step(i, more):
        for h in range(2):
            for d in range(2):
                ring_in(d, h, i).wait_recv()
                if more == 2 or (more == 1 and h == d):
                    ring(d, h, i + 1).start()
                sib(2 * i - d, step_slot(d, i), h).start()

    def block_slot(n):
        off = jnp.where(n % 2 == 1, (n + 1) // 2, NZ - n // 2)
        return (z + off) % NZ

    def blocks(n, carry):
        slot = block_slot(n)
        for h in range(2):
            sib_in(n, slot, h).wait_recv()
        for cs in range(2):
            s = cs * NZ + slot
            a = abuf[cs, slot].astype(F32)
            ssq[...] += a[:, :128] * a[:, :128] + a[:, 128:] * a[:, 128:]
            ag = (a * gain_row(s)).astype(BF16)
            acc[0:256, :] += lax.dot_general(ubuf[s], ag, (((0,), (1,)), ((), ())), preferred_element_type=F32)
        return carry

    def loop_step(i, carry):
        ring_step(i, 2)

        @pl.when(jnp.logical_not(mine))
        def _():
            for k in range(2):
                u_direct_in(2 * (i - 1) + k).wait_recv()
                u_mate(2 * (i - 1) + k).start()
        return carry

    lax.fori_loop(1, 5, loop_step, 0)
    ring_step(5, 2)

    @pl.when(jnp.logical_not(mine))
    def _():
        def wait_u(k, carry):
            u_mate_in(k).wait_recv()
            return carry

        lax.fori_loop(0, 8, wait_u, 0)

    @pl.when(mine)
    def _():
        u_local.wait()

    lax.fori_loop(0, 5, blocks, 0)
    ring_step(6, 2)
    lax.fori_loop(5, 10, blocks, 0)
    ring_step(7, 1)
    lax.fori_loop(10, 15, blocks, 0)
    for d in range(2):
        ring_in(d, d, 8).wait_recv()
        sib(15, (z + 8) % NZ, d).start()
    blocks(15, 0)

    t_copy.wait_recv()
    t2x = jnp.where(mine, tsrc[0:2, :], tbuf[0:2, :])
    tgt = jnp.concatenate([t2x[0:1, :], t2x[1:2, :], t2x[0:1, :], t2x[1:2, :]], axis=1)
    scale_row = jnp.where(lax.broadcasted_iota(jnp.int32, (1, 512), 1) < 256, scale_ref[0], scale_ref[1])
    mean_sq = jnp.sum(ssq[...].T, axis=0, keepdims=True) * (1.0 / 8192.0)
    r_row = lax.rsqrt(mean_sq + norm_eps)

    def as_tile(row):
        return [row[:, 128 * k:128 * k + 128] for k in range(4)]

    def lane_sum(row):
        return row[:, :128] + row[:, 128:256] + row[:, 256:384] + row[:, 384:]

    def is_target(plane):
        return lax.broadcasted_iota(jnp.int32, (256, 512), 0).astype(F32) == tgt - ((plane * NZ + z) * 256).astype(F32)

    logits = acc[0:256, :] * r_row
    m = jnp.max(logits, axis=0, keepdims=True)
    ex = jnp.exp(logits - m)
    acc[0:256, :] = ex
    acc[256:264, :] = jnp.broadcast_to(m, (8, 512))
    part_lse = m + jnp.log(jnp.sum(ex, axis=0, keepdims=True))
    part_t = lane_sum(jnp.sum(jnp.where(is_target(c), logits, 0.0), axis=0, keepdims=True) * scale_row)
    zst[z] = jnp.concatenate(as_tile(part_lse) + [part_t] * 4, axis=0)

    def z_copy(k):
        return rcopy(zst.at[z], zst.at[z], z_s.at[k], z_r.at[k], dev(x, y, (z + k) % NZ, c))

    def z_in(k):
        slot = (z + NZ - k) % NZ
        return rcopy(zst.at[slot], zst.at[slot], z_s.at[k], z_r.at[k], dev(x, y, (z + k) % NZ, c))

    def z_all(act):
        def body(k, carry):
            act(k)
            return carry

        lax.fori_loop(1, NZ, body, 0)

    z_all(lambda k: z_copy(k).start())
    lg_copy = rcopy(acc, accb, lg_sem.at[0], lg_sem.at[1], sibling)
    lg_copy.start()
    weight = scale_row * r_row
    z_all(lambda k: z_in(k).wait_recv())

    st = zst[...]
    l16 = st[:, 0:4, :]
    top = jnp.max(l16, axis=0)
    plane_lse = top + jnp.log(jnp.sum(jnp.exp(l16 - top[None]), axis=0))
    lebuf[c] = jnp.concatenate([plane_lse, jnp.sum(st[:, 4:8, :], axis=0)], axis=0)
    le_copy = rcopy(lebuf.at[c], lebuf.at[c], le_sem.at[0], le_sem.at[1], sibling)
    le_in = rcopy(lebuf.at[1 - c], lebuf.at[1 - c], le_sem.at[0], le_sem.at[1], sibling)
    le_copy.start()
    lg_copy.wait_recv()
    le_in.wait_recv()
    l_a, l_b = lebuf[0, 0:4, :], lebuf[1, 0:4, :]
    l_top = jnp.maximum(l_a, l_b)
    lse = l_top + jnp.log(jnp.exp(l_a - l_top) + jnp.exp(l_b - l_top))
    lse_row = jnp.concatenate([lse[k:k + 1, :] for k in range(4)], axis=1)

    def gradient(plane, buf):
        share = jnp.exp(buf[256:257, :] - lse_row)
        gbuf[plane] = (weight * (buf[0:256, :] * share - is_target(plane).astype(F32))).astype(BF16)

    gradient(c, acc)
    gradient(1 - c, accb)

    def l_copy(axis, k):
        if axis == 0:
            return rcopy(lx.at[x], lx.at[x], l_s.at[0, k], l_r.at[0, k], dev((x + k) % 4, y, z, c))
        return rcopy(ly.at[y], ly.at[y], l_s.at[1, k], l_r.at[1, k], dev(x, (y + k) % 4, z, c))

    def l_in(axis, k):
        if axis == 0:
            slot = (x + 4 - k) % 4
            return rcopy(lx.at[slot], lx.at[slot], l_s.at[0, k], l_r.at[0, k], dev((x + k) % 4, y, z, c))
        slot = (y + 4 - k) % 4
        return rcopy(ly.at[slot], ly.at[slot], l_s.at[1, k], l_r.at[1, k], dev(x, (y + k) % 4, z, c))

    def loss_x():
        lx[x] = jnp.broadcast_to(lane_sum(scale_row * lse_row), (8, 128)) - (
            jnp.broadcast_to(lebuf[0, 4:5, :], (8, 128)) + jnp.broadcast_to(lebuf[1, 4:5, :], (8, 128)))
        for k in range(1, 4):
            l_copy(0, k).start()

    def loss_y():
        for k in range(1, 4):
            l_in(0, k).wait_recv()
        ly[y] = lx[0] + lx[1] + lx[2] + lx[3]
        for k in range(1, 4):
            l_copy(1, k).start()

    def loss_end():
        for k in range(1, 4):
            l_in(1, k).wait_recv()
        tot = ly[0] + ly[1] + ly[2] + ly[3]
        loss_ref[0] = jnp.sum(tot[0:1, :]) * (1.0 / 4096.0)

    def along(axis, step):
        if axis == 0:
            return dev((x + step) % 4, y, z, c)
        return dev(x, (y + step) % 4, z, c)

    def grad_block(dy, dx):
        y_, x_ = (y + dy) % 4, (x + dx) % 4
        s = ((y_ * 2 + x_ % 2) * 2 + c) * 2
        plane, slot = s // NZ, s % NZ
        for k in range(2):
            pbuf[y_, x_, :, 256 * k:256 * k + 256] = jnp.dot(
                gbuf[x_ // 2], abuf[plane, slot + k], preferred_element_type=F32).astype(BF16)

    def blk(axis, step, o):
        if axis == 0:
            return pbuf.at[(y + o) % 4, (x + step) % 4]
        return pbuf.at[(y + step) % 4, (x + o) % 4]

    def part(axis, which):
        return pl.ds(128 * axis + 64 * which, 64)

    STEP = (1, 3)

    def send_o(axis, d, o):
        return rcopy(blk(axis, 2, o).at[part(axis, d)], r_o.at[axis, d, o], rs_s.at[0, axis, d, o], rs_r.at[0, axis, d, o], along(axis, STEP[d]))

    def send_d(axis, d, o):
        return rcopy(blk(axis, STEP[d], o).at[part(axis, 1 - d)], r_d.at[axis, d, o], rs_s.at[1, axis, d, o], rs_r.at[1, axis, d, o], along(axis, STEP[d]))

    def send_c(axis, d, o):
        return rcopy(blk(axis, STEP[d], o).at[part(axis, d)], r_c.at[axis, d, o], rs_s.at[2, axis, d, o], rs_r.at[2, axis, d, o], along(axis, STEP[d]))

    def send_o2(axis, d):
        return rcopy(blk(axis, 0, 2).at[part(axis, d)], q_o.at[axis, d], qs_s.at[0, axis, d], qs_r.at[0, axis, d], along(1 - axis, STEP[d]))

    def send_d2(axis, d):
        return rcopy(blk(axis, 0, STEP[d]).at[part(axis, 1 - d)], q_d.at[axis, d], qs_s.at[1, axis, d], qs_r.at[1, axis, d], along(1 - axis, STEP[d]))

    def send_c2(axis, d):
        return rcopy(blk(axis, 0, STEP[d]).at[part(axis, d)], q_c.at[axis, d], qs_s.at[2, axis, d], qs_r.at[2, axis, d], along(1 - axis, STEP[d]))

    def start_o(axis, o):
        for d in range(2):
            send_o(axis, d, o).start()

    def start_d(axis, o):
        for d in range(2):
            send_d(axis, d, o).start()

    def pair_sum(axis, d, o):
        send_o(axis, d, o).wait_recv()
        ref = blk(axis, STEP[d], o)
        rows = part(axis, d)
        ref[rows, :] = ref[rows, :] + r_o[axis, d, o]
        send_c(axis, d, o).start()

    def pair_sums(o):
        for axis in range(2):
            for d in range(2):
                pair_sum(axis, d, o)

    def first_pass(o):
        for axis in range(2):
            own = blk(axis, 0, o)
            for w in range(2):
                send_c(axis, w, o).wait_recv()
                send_d(axis, 1 - w, o).wait_recv()
                rows = part(axis, w)
                total = own[rows, :].astype(F32) + r_c[axis, w, o].astype(F32) + r_d[axis, 1 - w, o].astype(F32)
                if o == 0:
                    fin[rows, :] = total
                else:
                    own[rows, :] = total.astype(BF16)
                if o == 2:
                    send_o2(axis, w).start()
            if o in STEP:
                send_d2(axis, STEP.index(o)).start()

    def both(start, o):
        for axis in range(2):
            start(axis, o)

    grad_block(2, 2)
    both(start_o, 2)
    for o in (1, 3, 0):
        grad_block(o, 2)
        start_o(0, o)
        grad_block(2, o)
        start_o(1, o)
    both(start_d, 2)
    loss_x()
    pair_sums(2)
    for dy in (1, 3):
        for dx in (1, 3):
            grad_block(dy, dx)
    both(start_d, 1)
    both(start_d, 3)
    pair_sums(1)
    pair_sums(3)
    first_pass(2)
    for k in (1, 3):
        grad_block(0, k)
        grad_block(k, 0)
    both(start_d, 0)
    pair_sums(0)
    loss_y()
    first_pass(1)
    first_pass(3)
    grad_block(0, 0)
    for axis in range(2):
        for d in range(2):
            send_o2(axis, d).wait_recv()
            ref = blk(axis, 0, STEP[d])
            rows = part(axis, d)
            ref[rows, :] = ref[rows, :] + q_o[axis, d]
            send_c2(axis, d).start()
    first_pass(0)
    s_own = ((y * 2 + xl) * 2 + c) * 2
    gain_own = jnp.concatenate([gain_row(s_own), gain_row(s_own + 1)], axis=1)
    for axis in range(2):
        for w in range(2):
            send_c2(axis, w).wait_recv()
            send_d2(axis, 1 - w).wait_recv()
            rows = part(axis, w)
            fin[rows, :] = (fin[rows, :] + q_c[axis, w].astype(F32) + q_d[axis, 1 - w].astype(F32)) * gain_own
        o_ref[:, 128 * axis:128 * axis + 128] = fin[pl.ds(128 * axis, 128), :].T

    loss_end()

    for axis in range(2):
        for d in range(2):
            for o in range(4):
                send_o(axis, d, o).wait_send()
                send_d(axis, d, o).wait_send()
                send_c(axis, d, o).wait_send()
            send_o2(axis, d).wait_send()
            send_d2(axis, d).wait_send()
            send_c2(axis, d).wait_send()
    for axis in range(2):
        for k in range(1, 4):
            l_copy(axis, k).wait_send()
    for copy in (t_copy, lg_copy, le_copy):
        copy.wait_send()

    z_all(lambda k: z_copy(k).wait_send())

    def ring_done(i, carry):
        for h in range(2):
            for d in range(2):
                ring(d, h, i).wait_send()
        return carry

    lax.fori_loop(1, 8, ring_done, 0)
    for d in range(2):
        ring(d, d, 8).wait_send()

    def sib_done(n, carry):
        for h in range(2):
            sib(n, block_slot(n), h).wait_send()
        return carry

    lax.fori_loop(0, 16, sib_done, 0)

    @pl.when(mine)
    def _():
        def done(k, carry):
            u_direct(k).wait_send()
            return carry

        lax.fori_loop(0, 8, done, 0)

    @pl.when(jnp.logical_not(mine))
    def _():
        for h in range(2):
            swap(h).wait_send()

        def done(k, carry):
            u_mate(k).wait_send()
            return carry

        lax.fori_loop(0, 8, done, 0)


def per_device(hidden_states, exit_layers, targets, norm_gain, exit_scale, unembedding):
    vmem = pl.BlockSpec(memory_space=pltpu.VMEM)
    smem = pl.BlockSpec(memory_space=pltpu.SMEM)
    anywhere = pl.BlockSpec(memory_space=pltpu.HBM)
    dma = pltpu.SemaphoreType.DMA
    grad, loss = pl.pallas_call(
        kernel,
        out_shape=(jax.ShapeDtypeStruct((512, 256), F32), jax.ShapeDtypeStruct((1,), F32)),
        in_specs=[anywhere] * 6,
        out_specs=(vmem, smem),
        scratch_shapes=[
            pltpu.SMEM((2, 4), jnp.int32), pltpu.SMEM((2,), F32), pltpu.VMEM((2, 128), jnp.int32),
            pltpu.VMEM((64, 128), BF16),
            pltpu.VMEM((4, 256, 256), BF16),
            pltpu.VMEM((512, 256), BF16),
            pltpu.VMEM((8, 128), F32),
            pltpu.VMEM((64, 128), F32),
            dma((5,)),
            pltpu.VMEM((2, 16, 512, 256), BF16),
            pltpu.VMEM((32, 256, 256), BF16),
            pltpu.VMEM((264, 512), F32),
            pltpu.VMEM((264, 512), F32),
            pltpu.VMEM((512, 128), F32),
            pltpu.VMEM((2, 256, 512), BF16),
            pltpu.VMEM((8, 128), F32),
            pltpu.VMEM((16, 8, 128), F32),
            pltpu.VMEM((2, 8, 128), F32),
            pltpu.VMEM((4, 8, 128), F32),
            pltpu.VMEM((4, 8, 128), F32),
            pltpu.VMEM((4, 4, 256, 512), BF16),
            pltpu.VMEM((256, 512), F32),
            pltpu.VMEM((2, 2, 4, 64, 512), BF16),
            pltpu.VMEM((2, 2, 4, 64, 512), BF16),
            pltpu.VMEM((2, 2, 4, 64, 512), BF16),
            pltpu.VMEM((2, 2, 64, 512), BF16),
            pltpu.VMEM((2, 2, 64, 512), BF16),
            pltpu.VMEM((2, 2, 64, 512), BF16),
            dma((2, 2)), dma((2, 2, 8)), dma((2, 2, 8)), dma((16, 2)), dma((16, 2)),
            dma((2, 8)), dma((2, 8)), dma, dma((2,)), dma((2,)), dma((16,)), dma((16,)), dma((2,)),
            dma((2, 4)), dma((2, 4)), dma((3, 2, 2, 4)), dma((3, 2, 2, 4)), dma((3, 2, 2)), dma((3, 2, 2)),
        ],
        compiler_params=pltpu.CompilerParams(
            collective_id=0, has_side_effects=True, vmem_limit_bytes=30 << 20),
    )(*[pltpu.with_memory_space_constraint(a, pltpu.HBM) for a in (
        exit_layers.T, exit_scale, hidden_states, unembedding.reshape(32, 256, 256),
        targets.reshape(2, 128), norm_gain.reshape(64, 128))])
    return (grad, loss.reshape(()))


def solution(mesh):
    in_specs = (P(None, "dp", "vocab"), P("dp", None), P("dp"), P(), P(), P(None, "vocab"))
    out_specs = (P("dp", "vocab"), P())
    return jax.shard_map(
        per_device, mesh=mesh, in_specs=in_specs, out_specs=out_specs, check_vma=False
    )
```

```python
import jax
import jax.numpy as jnp
from jax import lax
from jax.experimental import pallas as pl
from jax.experimental.pallas import tpu as pltpu
from jax.sharding import PartitionSpec as P

norm_eps = 1e-05
MESH = pl.DeviceIdType.MESH
F32 = jnp.float32
BF16 = jnp.bfloat16
NZ, NX, NY = 16, 4, 4


def kernel(el_any, scale_any, hid_ref, u_ref, tgt_any, gain_any, o_ref, loss_ref,
           el_ref, scale_ref, tgt_ref, gain_ref, hbuf, xbuf, tsrc, gain, in_sem,
           abuf, ubuf, acc, ssq, gbuf, tbuf, zst, lebuf, lx, ly, pbuf, fin,
           r_o, r_d, r_c, q_o, q_d, q_c,
           swap_sem, ring_s, ring_r, sib_s, sib_r, u_s, u_r, u_loc, t_sem, lg_sem, z_s, z_r, le_sem,
           l_s, l_r, rs_s, rs_r, qs_s, qs_r):
    dp = lax.axis_index("dp")
    vo = lax.axis_index("vocab")
    c = dp % 2
    xl = (dp // 2) % 2
    y = dp // 4
    z = vo % NZ
    xh = vo // NZ
    x = xh * 2 + xl

    def dev(x_, y_, z_, c_):
        return ((y_ * 2 + x_ % 2) * 2 + c_, (x_ // 2) * NZ + z_)

    sibling = dev(x, y, z, 1 - c)
    partner = dev((x + 2) % 4, y, z, 1 - c)

    def rcopy(src, dst, s, r, to):
        return pltpu.make_async_remote_copy(src_ref=src, dst_ref=dst, send_sem=s, recv_sem=r,
                                            device_id=to, device_id_type=MESH)

    inputs = [pltpu.make_async_copy(a, b, in_sem.at[k]) for k, (a, b) in enumerate((
        (hid_ref, hbuf), (el_any, el_ref), (scale_any, scale_ref), (tgt_any, tgt_ref), (gain_any, gain_ref)))]
    for copy in inputs[:2]:
        copy.start()

    bar = pltpu.get_barrier_semaphore()
    for to in (sibling, partner, dev(x, y, (z + 1) % NZ, c), dev(x, y, (z + NZ - 1) % NZ, c)):
        pl.semaphore_signal(bar, inc=1, device_id=to, device_id_type=MESH)
    for k in range(1, 4):
        pl.semaphore_signal(bar, inc=1, device_id=dev((x + k) % 4, y, z, c), device_id_type=MESH)
        pl.semaphore_signal(bar, inc=1, device_id=dev(x, (y + k) % 4, z, c), device_id_type=MESH)

    for copy in inputs[2:]:
        copy.start()

    def select(dst):
        for e in range(2):
            for row in range(4):
                dst[pl.ds(256 * e + 64 * row, 64), :] = hbuf[el_ref[e, row], pl.ds(64 * row, 64), :]

    mine = c == xh
    for copy in inputs[:2]:
        copy.wait()

    @pl.when(mine)
    def _():
        select(abuf.at[c, z])

    @pl.when(jnp.logical_not(mine))
    def _():
        select(xbuf)

    pl.semaphore_wait(bar, 10)

    def swap(h):
        rows = pl.ds(256 * h, 256)
        return rcopy(xbuf.at[rows], abuf.at[1 - c, z, rows], swap_sem.at[0, h], swap_sem.at[1, h], partner)

    def swap_in(h):
        ref = abuf.at[c, z, pl.ds(256 * h, 256)]
        return rcopy(ref, ref, swap_sem.at[0, h], swap_sem.at[1, h], partner)

    def u_direct(k):
        j = (1 - xl) * 8 + k
        return rcopy(u_ref.at[pl.ds(2 * j, 2)], ubuf.at[pl.ds(2 * j, 2)], u_s.at[0, k], u_r.at[0, k], dev(3 - x, y, z, c))

    def u_direct_in(k):
        j = xl * 8 + k
        return rcopy(ubuf.at[pl.ds(2 * j, 2)], ubuf.at[pl.ds(2 * j, 2)], u_s.at[0, k], u_r.at[0, k], dev(3 - x, y, z, c))

    def u_mate(k):
        j = xl * 8 + k
        return rcopy(ubuf.at[pl.ds(2 * j, 2)], ubuf.at[pl.ds(2 * j, 2)], u_s.at[1, k], u_r.at[1, k], dev(xh * 2 + 1 - xl, y, z, c))

    def u_mate_in(k):
        j = (1 - xl) * 8 + k
        return rcopy(ubuf.at[pl.ds(2 * j, 2)], ubuf.at[pl.ds(2 * j, 2)], u_s.at[1, k], u_r.at[1, k], dev(xh * 2 + 1 - xl, y, z, c))

    u_local = pltpu.make_async_copy(u_ref, ubuf, u_loc)

    @pl.when(jnp.logical_not(mine))
    def _():
        for h in range(2):
            swap(h).start()

    def step_slot(d, i):
        return (z - i + NZ) % NZ if d == 0 else (z + i) % NZ

    def half(slot, h):
        return abuf.at[c, slot, pl.ds(256 * h, 256)]

    def ring(d, h, i):
        ref = half(step_slot(d, i - 1), h)
        to = dev(x, y, (z + 1) % NZ, c) if d == 0 else dev(x, y, (z + NZ - 1) % NZ, c)
        return rcopy(ref, ref, ring_s.at[d, h, i - 1], ring_r.at[d, h, i - 1], to)

    def ring_in(d, h, i):
        ref = half(step_slot(d, i), h)
        to = dev(x, y, (z + 1) % NZ, c) if d == 0 else dev(x, y, (z + NZ - 1) % NZ, c)
        return rcopy(ref, ref, ring_s.at[d, h, i - 1], ring_r.at[d, h, i - 1], to)

    def sib(n, slot):
        ref = abuf.at[c, slot]
        return rcopy(ref, ref, sib_s.at[n], sib_r.at[n], sibling)

    def sib_in(n, slot):
        ref = abuf.at[1 - c, slot]
        return rcopy(ref, ref, sib_s.at[n], sib_r.at[n], sibling)

    for h in range(2):
        @pl.when(jnp.logical_not(mine))
        def _():
            swap_in(h).wait_recv()

        for d in range(2):
            ring(d, h, 1).start()
    sib(0, z).start()

    for copy in inputs[2:]:
        copy.wait()
    tsrc[0:2, :] = tgt_ref[...].astype(F32)
    t_copy = rcopy(tsrc, tbuf, t_sem.at[0], t_sem.at[1], sibling)
    t_copy.start()

    @pl.when(mine)
    def _():
        def send_u(k, carry):
            u_direct(k).start()
            return carry

        lax.fori_loop(0, 8, send_u, 0)
        u_local.start()


    gain[...] = gain_ref[...].astype(F32)

    def gain_row(s):
        return jnp.concatenate([gain[pl.ds(2 * s, 1), :], gain[pl.ds(2 * s + 1, 1), :]], axis=1)

    acc[c, 0:256, :] = jnp.zeros((256, 512), F32)
    ssq[...] = jnp.zeros_like(ssq)

    def ring_step(i, more):
        for h in range(2):
            for d in range(2):
                ring_in(d, h, i).wait_recv()
                if more == 2 or (more == 1 and h == d):
                    ring(d, h, i + 1).start()
        for d in range(2):
            sib(2 * i - d, step_slot(d, i)).start()

    def block_slot(n):
        off = jnp.where(n % 2 == 1, (n + 1) // 2, NZ - n // 2)
        return (z + off) % NZ

    def blocks(n, carry):
        slot = block_slot(n)
        sib_in(n, slot).wait_recv()
        for cs in range(2):
            s = cs * NZ + slot
            a = abuf[cs, slot].astype(F32)
            ssq[...] += a[:, :128] * a[:, :128] + a[:, 128:] * a[:, 128:]
            ag = (a * gain_row(s)).astype(BF16)
            acc[c, 0:256, :] += lax.dot_general(ubuf[s], ag, (((0,), (1,)), ((), ())), preferred_element_type=F32)
        return carry

    def loop_step(i, carry):
        ring_step(i, 2)

        @pl.when(jnp.logical_not(mine))
        def _():
            for k in range(2):
                u_direct_in(2 * (i - 1) + k).wait_recv()
                u_mate(2 * (i - 1) + k).start()
        return carry

    lax.fori_loop(1, 5, loop_step, 0)
    ring_step(5, 2)

    @pl.when(jnp.logical_not(mine))
    def _():
        def wait_u(k, carry):
            u_mate_in(k).wait_recv()
            return carry

        lax.fori_loop(0, 8, wait_u, 0)

    @pl.when(mine)
    def _():
        u_local.wait()

    lax.fori_loop(0, 5, blocks, 0)
    ring_step(6, 2)
    lax.fori_loop(5, 10, blocks, 0)
    ring_step(7, 1)
    lax.fori_loop(10, 15, blocks, 0)
    for d in range(2):
        ring_in(d, d, 8).wait_recv()
    sib(15, (z + 8) % NZ).start()
    blocks(15, 0)

    def gather_done():
        def ring_done(i, carry):
            for h in range(2):
                for d in range(2):
                    ring(d, h, i).wait_send()
            return carry

        lax.fori_loop(1, 8, ring_done, 0)
        for d in range(2):
            ring(d, d, 8).wait_send()

        def sib_done(n, carry):
            sib(n, block_slot(n)).wait_send()
            return carry

        lax.fori_loop(0, 16, sib_done, 0)

        @pl.when(mine)
        def _():
            def done(k, carry):
                u_direct(k).wait_send()
                return carry

            lax.fori_loop(0, 8, done, 0)

        @pl.when(jnp.logical_not(mine))
        def _():
            for h in range(2):
                swap(h).wait_send()

            def done(k, carry):
                u_mate(k).wait_send()
                return carry

            lax.fori_loop(0, 8, done, 0)

    t_copy.wait_recv()
    t2x = jnp.where(mine, tsrc[0:2, :], tbuf[0:2, :])
    tgt = jnp.concatenate([t2x[0:1, :], t2x[1:2, :], t2x[0:1, :], t2x[1:2, :]], axis=1)
    scale_row = jnp.where(lax.broadcasted_iota(jnp.int32, (1, 512), 1) < 256, scale_ref[0], scale_ref[1])
    mean_sq = jnp.sum(ssq[...].T, axis=0, keepdims=True) * (1.0 / 8192.0)
    r_row = lax.rsqrt(mean_sq + norm_eps)

    def as_tile(row):
        return [row[:, 128 * k:128 * k + 128] for k in range(4)]

    def lane_sum(row):
        return row[:, :128] + row[:, 128:256] + row[:, 256:384] + row[:, 384:]

    def is_target(plane):
        return lax.broadcasted_iota(jnp.int32, (256, 512), 0).astype(F32) == tgt - ((plane * NZ + z) * 256).astype(F32)

    logits = acc[c, 0:256, :] * r_row
    m = jnp.max(logits, axis=0, keepdims=True)
    ex = jnp.exp(logits - m)
    acc[c, 0:256, :] = ex
    acc[c, 256:264, :] = jnp.broadcast_to(m, (8, 512))
    part_lse = m + jnp.log(jnp.sum(ex, axis=0, keepdims=True))
    part_t = lane_sum(jnp.sum(jnp.where(is_target(c), logits, 0.0), axis=0, keepdims=True) * scale_row)
    zst[z] = jnp.concatenate(as_tile(part_lse) + [part_t] * 4, axis=0)

    def z_copy(k):
        return rcopy(zst.at[z], zst.at[z], z_s.at[k], z_r.at[k], dev(x, y, (z + k) % NZ, c))

    def z_in(k):
        slot = (z + NZ - k) % NZ
        return rcopy(zst.at[slot], zst.at[slot], z_s.at[k], z_r.at[k], dev(x, y, (z + k) % NZ, c))

    def z_all(act):
        def body(k, carry):
            act(k)
            return carry

        lax.fori_loop(1, NZ, body, 0)

    z_all(lambda k: z_copy(k).start())
    lg_copy = rcopy(acc.at[c], acc.at[c], lg_sem.at[0], lg_sem.at[1], sibling)
    lg_in = rcopy(acc.at[1 - c], acc.at[1 - c], lg_sem.at[0], lg_sem.at[1], sibling)
    lg_copy.start()
    gather_done()
    weight = scale_row * r_row
    z_all(lambda k: z_in(k).wait_recv())

    st = zst[...]
    l16 = st[:, 0:4, :]
    top = jnp.max(l16, axis=0)
    plane_lse = top + jnp.log(jnp.sum(jnp.exp(l16 - top[None]), axis=0))
    lebuf[c] = jnp.concatenate([plane_lse, jnp.sum(st[:, 4:8, :], axis=0)], axis=0)
    le_copy = rcopy(lebuf.at[c], lebuf.at[c], le_sem.at[0], le_sem.at[1], sibling)
    le_in = rcopy(lebuf.at[1 - c], lebuf.at[1 - c], le_sem.at[0], le_sem.at[1], sibling)
    le_copy.start()
    lg_in.wait_recv()
    le_in.wait_recv()
    l_a, l_b = lebuf[0, 0:4, :], lebuf[1, 0:4, :]
    l_top = jnp.maximum(l_a, l_b)
    lse = l_top + jnp.log(jnp.exp(l_a - l_top) + jnp.exp(l_b - l_top))
    lse_row = jnp.concatenate([lse[k:k + 1, :] for k in range(4)], axis=1)

    def gradient(plane):
        share = jnp.exp(acc[plane, 256:257, :] - lse_row)
        gbuf[plane] = (weight * (acc[plane, 0:256, :] * share - is_target(plane).astype(F32))).astype(BF16)

    def l_copy(axis, k):
        if axis == 0:
            return rcopy(lx.at[x], lx.at[x], l_s.at[0, k], l_r.at[0, k], dev((x + k) % 4, y, z, c))
        return rcopy(ly.at[y], ly.at[y], l_s.at[1, k], l_r.at[1, k], dev(x, (y + k) % 4, z, c))

    def l_in(axis, k):
        if axis == 0:
            slot = (x + 4 - k) % 4
            return rcopy(lx.at[slot], lx.at[slot], l_s.at[0, k], l_r.at[0, k], dev((x + k) % 4, y, z, c))
        slot = (y + 4 - k) % 4
        return rcopy(ly.at[slot], ly.at[slot], l_s.at[1, k], l_r.at[1, k], dev(x, (y + k) % 4, z, c))

    def loss_x():
        lx[x] = jnp.broadcast_to(lane_sum(scale_row * lse_row), (8, 128)) - (
            jnp.broadcast_to(lebuf[0, 4:5, :], (8, 128)) + jnp.broadcast_to(lebuf[1, 4:5, :], (8, 128)))
        for k in range(1, 4):
            l_copy(0, k).start()

    def loss_y():
        for k in range(1, 4):
            l_in(0, k).wait_recv()
        ly[y] = lx[0] + lx[1] + lx[2] + lx[3]
        for k in range(1, 4):
            l_copy(1, k).start()

    def loss_end():
        for k in range(1, 4):
            l_in(1, k).wait_recv()
        tot = ly[0] + ly[1] + ly[2] + ly[3]
        loss_ref[0] = jnp.sum(tot[0:1, :]) * (1.0 / 4096.0)

    def along(axis, step):
        if axis == 0:
            return dev((x + step) % 4, y, z, c)
        return dev(x, (y + step) % 4, z, c)

    def grad_block(dy, dx):
        y_, x_ = (y + dy) % 4, (x + dx) % 4
        s = ((y_ * 2 + x_ % 2) * 2 + c) * 2
        plane, slot = s // NZ, s % NZ
        for k in range(2):
            pbuf[y_, x_, :, 256 * k:256 * k + 256] = jnp.dot(
                gbuf[x_ // 2], abuf[plane, slot + k], preferred_element_type=F32).astype(BF16)

    def blk(axis, step, o):
        if axis == 0:
            return pbuf.at[(y + o) % 4, (x + step) % 4]
        return pbuf.at[(y + step) % 4, (x + o) % 4]

    def part(axis, which):
        return pl.ds(128 * axis + 64 * which, 64)

    STEP = (1, 3)

    def send_o(axis, d, o):
        return rcopy(blk(axis, 2, o).at[part(axis, d)], r_o.at[axis, d, o], rs_s.at[0, axis, d, o], rs_r.at[0, axis, d, o], along(axis, STEP[d]))

    def send_d(axis, d, o):
        return rcopy(blk(axis, STEP[d], o).at[part(axis, 1 - d)], r_d.at[axis, d, o], rs_s.at[1, axis, d, o], rs_r.at[1, axis, d, o], along(axis, STEP[d]))

    def send_c(axis, d, o):
        return rcopy(blk(axis, STEP[d], o).at[part(axis, d)], r_c.at[axis, d, o], rs_s.at[2, axis, d, o], rs_r.at[2, axis, d, o], along(axis, STEP[d]))

    def send_o2(axis, d):
        return rcopy(blk(axis, 0, 2).at[part(axis, d)], q_o.at[axis, d], qs_s.at[0, axis, d], qs_r.at[0, axis, d], along(1 - axis, STEP[d]))

    def send_d2(axis, d):
        return rcopy(blk(axis, 0, STEP[d]).at[part(axis, 1 - d)], q_d.at[axis, d], qs_s.at[1, axis, d], qs_r.at[1, axis, d], along(1 - axis, STEP[d]))

    def send_c2(axis, d):
        return rcopy(blk(axis, 0, STEP[d]).at[part(axis, d)], q_c.at[axis, d], qs_s.at[2, axis, d], qs_r.at[2, axis, d], along(1 - axis, STEP[d]))

    def start_o(axis, o):
        for d in range(2):
            send_o(axis, d, o).start()

    def start_d(axis, o):
        for d in range(2):
            send_d(axis, d, o).start()

    def pair_sum(axis, d, o):
        send_o(axis, d, o).wait_recv()
        ref = blk(axis, STEP[d], o)
        rows = part(axis, d)
        ref[rows, :] = ref[rows, :] + r_o[axis, d, o]
        send_c(axis, d, o).start()

    def pair_sums(o):
        for axis in range(2):
            for d in range(2):
                pair_sum(axis, d, o)

    def first_pass(o):
        for axis in range(2):
            own = blk(axis, 0, o)
            for w in range(2):
                send_c(axis, w, o).wait_recv()
                send_d(axis, 1 - w, o).wait_recv()
                rows = part(axis, w)
                total = own[rows, :].astype(F32) + r_c[axis, w, o].astype(F32) + r_d[axis, 1 - w, o].astype(F32)
                if o == 0:
                    fin[rows, :] = total
                else:
                    own[rows, :] = total.astype(BF16)
                if o == 2:
                    send_o2(axis, w).start()
            if o in STEP:
                send_d2(axis, STEP.index(o)).start()

    def both(start, o):
        for axis in range(2):
            start(axis, o)

    gradient(1 - xh)
    grad_block(2, 2)
    both(start_o, 2)
    for o in (1, 3, 0):
        grad_block(o, 2)
        start_o(0, o)
    gradient(xh)
    for o in (1, 3, 0):
        grad_block(2, o)
        start_o(1, o)
    both(start_d, 2)
    loss_x()
    pair_sums(2)
    for dy in (1, 3):
        for dx in (1, 3):
            grad_block(dy, dx)
    both(start_d, 1)
    both(start_d, 3)
    pair_sums(1)
    pair_sums(3)
    first_pass(2)
    for k in (1, 3):
        grad_block(0, k)
        grad_block(k, 0)
    both(start_d, 0)
    pair_sums(0)
    loss_y()
    first_pass(1)
    first_pass(3)
    grad_block(0, 0)
    for axis in range(2):
        for d in range(2):
            send_o2(axis, d).wait_recv()
            ref = blk(axis, 0, STEP[d])
            rows = part(axis, d)
            ref[rows, :] = ref[rows, :] + q_o[axis, d]
            send_c2(axis, d).start()
    first_pass(0)
    loss_end()

    for axis in range(2):
        for d in range(2):
            for o in range(4):
                send_o(axis, d, o).wait_send()
                send_d(axis, d, o).wait_send()
                send_c(axis, d, o).wait_send()
        for k in range(1, 4):
            l_copy(axis, k).wait_send()
    for copy in (t_copy, lg_copy, le_copy):
        copy.wait_send()
    z_all(lambda k: z_copy(k).wait_send())

    s_own = ((y * 2 + xl) * 2 + c) * 2
    gain_own = jnp.concatenate([gain_row(s_own), gain_row(s_own + 1)], axis=1)
    for axis in range(2):
        for w in range(2):
            send_c2(axis, w).wait_recv()
            send_d2(axis, 1 - w).wait_recv()
            rows = part(axis, w)
            fin[rows, :] = (fin[rows, :] + q_c[axis, w].astype(F32) + q_d[axis, 1 - w].astype(F32)) * gain_own
        o_ref[:, 128 * axis:128 * axis + 128] = fin[pl.ds(128 * axis, 128), :].T

    for axis in range(2):
        for d in range(2):
            send_o2(axis, d).wait_send()
            send_d2(axis, d).wait_send()
            send_c2(axis, d).wait_send()


def per_device(hidden_states, exit_layers, targets, norm_gain, exit_scale, unembedding):
    vmem = pl.BlockSpec(memory_space=pltpu.VMEM)
    smem = pl.BlockSpec(memory_space=pltpu.SMEM)
    anywhere = pl.BlockSpec(memory_space=pltpu.HBM)
    dma = pltpu.SemaphoreType.DMA
    grad, loss = pl.pallas_call(
        kernel,
        out_shape=(jax.ShapeDtypeStruct((512, 256), F32), jax.ShapeDtypeStruct((1,), F32)),
        in_specs=[anywhere] * 6,
        out_specs=(vmem, smem),
        scratch_shapes=[
            pltpu.SMEM((2, 4), jnp.int32), pltpu.SMEM((2,), F32), pltpu.VMEM((2, 128), jnp.int32),
            pltpu.VMEM((64, 128), BF16),
            pltpu.VMEM((4, 256, 256), BF16),
            pltpu.VMEM((512, 256), BF16),
            pltpu.VMEM((8, 128), F32),
            pltpu.VMEM((64, 128), F32),
            dma((5,)),
            pltpu.VMEM((2, 16, 512, 256), BF16),
            pltpu.VMEM((32, 256, 256), BF16),
            pltpu.VMEM((2, 264, 512), F32),
            pltpu.VMEM((512, 128), F32),
            pltpu.VMEM((2, 256, 512), BF16),
            pltpu.VMEM((8, 128), F32),
            pltpu.VMEM((16, 8, 128), F32),
            pltpu.VMEM((2, 8, 128), F32),
            pltpu.VMEM((4, 8, 128), F32),
            pltpu.VMEM((4, 8, 128), F32),
            pltpu.VMEM((4, 4, 256, 512), BF16),
            pltpu.VMEM((256, 512), F32),
            pltpu.VMEM((2, 2, 4, 64, 512), BF16),
            pltpu.VMEM((2, 2, 4, 64, 512), BF16),
            pltpu.VMEM((2, 2, 4, 64, 512), BF16),
            pltpu.VMEM((2, 2, 64, 512), BF16),
            pltpu.VMEM((2, 2, 64, 512), BF16),
            pltpu.VMEM((2, 2, 64, 512), BF16),
            dma((2, 2)), dma((2, 2, 8)), dma((2, 2, 8)), dma((16,)), dma((16,)),
            dma((2, 8)), dma((2, 8)), dma, dma((2,)), dma((2,)), dma((16,)), dma((16,)), dma((2,)),
            dma((2, 4)), dma((2, 4)), dma((3, 2, 2, 4)), dma((3, 2, 2, 4)), dma((3, 2, 2)), dma((3, 2, 2)),
        ],
        compiler_params=pltpu.CompilerParams(
            collective_id=0, has_side_effects=True, vmem_limit_bytes=30 << 20),
    )(*[pltpu.with_memory_space_constraint(a, pltpu.HBM) for a in (
        exit_layers.T, exit_scale, hidden_states, unembedding.reshape(32, 256, 256),
        targets.reshape(2, 128), norm_gain.reshape(64, 128))])
    return (grad, loss.reshape(()))


def solution(mesh):
    in_specs = (P(None, "dp", "vocab"), P("dp", None), P("dp"), P(), P(), P(None, "vocab"))
    out_specs = (P("dp", "vocab"), P())
    return jax.shard_map(
        per_device, mesh=mesh, in_specs=in_specs, out_specs=out_specs, check_vma=False
    )
```

```python
import jax
import jax.numpy as jnp
from jax import lax
from jax.experimental import pallas as pl
from jax.experimental.pallas import tpu as pltpu
from jax.sharding import PartitionSpec as P

norm_eps = 1e-05
MESH = pl.DeviceIdType.MESH
F32 = jnp.float32
BF16 = jnp.bfloat16
NZ, NX, NY = 16, 4, 4


def kernel(el_any, scale_any, hid_ref, u_ref, tgt_any, gain_any, o_ref, loss_ref,
           el_ref, scale_ref, tgt_ref, gain_ref, hbuf, xbuf, tsrc, gain, in_sem,
           abuf, ubuf, acc, ssq, gbuf, tbuf, zst, lebuf, lx, ly, pbuf, fin,
           r_o, r_d, r_c, q_o, q_d, q_c,
           swap_sem, ring_s, ring_r, sib_s, sib_r, u_s, u_r, u_loc, t_sem, lg_sem, z_s, z_r, le_sem,
           l_s, l_r, rs_s, rs_r, qs_s, qs_r):
    dp = lax.axis_index("dp")
    vo = lax.axis_index("vocab")
    c = dp % 2
    xl = (dp // 2) % 2
    y = dp // 4
    z = vo % NZ
    xh = vo // NZ
    x = xh * 2 + xl

    def dev(x_, y_, z_, c_):
        return ((y_ * 2 + x_ % 2) * 2 + c_, (x_ // 2) * NZ + z_)

    sibling = dev(x, y, z, 1 - c)
    partner = dev((x + 2) % 4, y, z, 1 - c)

    def rcopy(src, dst, s, r, to):
        return pltpu.make_async_remote_copy(src_ref=src, dst_ref=dst, send_sem=s, recv_sem=r,
                                            device_id=to, device_id_type=MESH)

    inputs = [pltpu.make_async_copy(a, b, in_sem.at[k]) for k, (a, b) in enumerate((
        (hid_ref, hbuf), (el_any, el_ref), (scale_any, scale_ref), (tgt_any, tgt_ref), (gain_any, gain_ref)))]
    for copy in inputs[:2]:
        copy.start()

    bar = pltpu.get_barrier_semaphore()
    for to in (sibling, partner, dev(x, y, (z + 1) % NZ, c), dev(x, y, (z + NZ - 1) % NZ, c)):
        pl.semaphore_signal(bar, inc=1, device_id=to, device_id_type=MESH)
    for k in range(1, 4):
        pl.semaphore_signal(bar, inc=1, device_id=dev((x + k) % 4, y, z, c), device_id_type=MESH)
        pl.semaphore_signal(bar, inc=1, device_id=dev(x, (y + k) % 4, z, c), device_id_type=MESH)

    for copy in inputs[2:]:
        copy.start()

    def select(dst):
        for e in range(2):
            for row in range(4):
                dst[pl.ds(256 * e + 64 * row, 64), :] = hbuf[el_ref[e, row], pl.ds(64 * row, 64), :]

    mine = c == xh
    for copy in inputs[:2]:
        copy.wait()

    @pl.when(mine)
    def _():
        select(abuf.at[c, z])

    @pl.when(jnp.logical_not(mine))
    def _():
        select(xbuf)

    pl.semaphore_wait(bar, 10)

    def swap(h):
        rows = pl.ds(256 * h, 256)
        return rcopy(xbuf.at[rows], abuf.at[1 - c, z, rows], swap_sem.at[0, h], swap_sem.at[1, h], partner)

    def swap_in(h):
        ref = abuf.at[c, z, pl.ds(256 * h, 256)]
        return rcopy(ref, ref, swap_sem.at[0, h], swap_sem.at[1, h], partner)

    def u_direct(k):
        j = (1 - xl) * 8 + k
        return rcopy(u_ref.at[pl.ds(2 * j, 2)], ubuf.at[pl.ds(2 * j, 2)], u_s.at[0, k], u_r.at[0, k], dev(3 - x, y, z, c))

    def u_direct_in(k):
        j = xl * 8 + k
        return rcopy(ubuf.at[pl.ds(2 * j, 2)], ubuf.at[pl.ds(2 * j, 2)], u_s.at[0, k], u_r.at[0, k], dev(3 - x, y, z, c))

    def u_mate(k):
        j = xl * 8 + k
        return rcopy(ubuf.at[pl.ds(2 * j, 2)], ubuf.at[pl.ds(2 * j, 2)], u_s.at[1, k], u_r.at[1, k], dev(xh * 2 + 1 - xl, y, z, c))

    def u_mate_in(k):
        j = (1 - xl) * 8 + k
        return rcopy(ubuf.at[pl.ds(2 * j, 2)], ubuf.at[pl.ds(2 * j, 2)], u_s.at[1, k], u_r.at[1, k], dev(xh * 2 + 1 - xl, y, z, c))

    u_local = pltpu.make_async_copy(u_ref, ubuf, u_loc)

    @pl.when(jnp.logical_not(mine))
    def _():
        for h in range(2):
            swap(h).start()

    def step_slot(d, i):
        return (z - i + NZ) % NZ if d == 0 else (z + i) % NZ

    def half(slot, h):
        return abuf.at[c, slot, pl.ds(256 * h, 256)]

    def ring(d, h, i):
        ref = half(step_slot(d, i - 1), h)
        to = dev(x, y, (z + 1) % NZ, c) if d == 0 else dev(x, y, (z + NZ - 1) % NZ, c)
        return rcopy(ref, ref, ring_s.at[d, h, i - 1], ring_r.at[d, h, i - 1], to)

    def ring_in(d, h, i):
        ref = half(step_slot(d, i), h)
        to = dev(x, y, (z + 1) % NZ, c) if d == 0 else dev(x, y, (z + NZ - 1) % NZ, c)
        return rcopy(ref, ref, ring_s.at[d, h, i - 1], ring_r.at[d, h, i - 1], to)

    def sib(n, slot):
        ref = abuf.at[c, slot]
        return rcopy(ref, ref, sib_s.at[n], sib_r.at[n], sibling)

    def sib_in(n, slot):
        ref = abuf.at[1 - c, slot]
        return rcopy(ref, ref, sib_s.at[n], sib_r.at[n], sibling)

    for h in range(2):
        @pl.when(jnp.logical_not(mine))
        def _():
            swap_in(h).wait_recv()

        for d in range(2):
            ring(d, h, 1).start()
    sib(0, z).start()

    for copy in inputs[2:]:
        copy.wait()
    tsrc[0:2, :] = tgt_ref[...].astype(F32)
    t_copy = rcopy(tsrc, tbuf, t_sem.at[0], t_sem.at[1], sibling)
    t_copy.start()

    @pl.when(mine)
    def _():
        def send_u(k, carry):
            u_direct(k).start()
            return carry

        lax.fori_loop(0, 8, send_u, 0)
        u_local.start()


    gain[...] = gain_ref[...].astype(F32)

    def gain_row(s):
        return jnp.concatenate([gain[pl.ds(2 * s, 1), :], gain[pl.ds(2 * s + 1, 1), :]], axis=1)

    acc[c, 0:256, :] = jnp.zeros((256, 512), F32)
    ssq[...] = jnp.zeros_like(ssq)

    def ring_step(i, more):
        for h in range(2):
            for d in range(2):
                ring_in(d, h, i).wait_recv()
                if more == 2 or (more == 1 and h == d):
                    ring(d, h, i + 1).start()
        for d in range(2):
            sib(2 * i - d, step_slot(d, i)).start()

    def block_slot(n):
        off = jnp.where(n % 2 == 1, (n + 1) // 2, NZ - n // 2)
        return (z + off) % NZ

    def blocks(n, carry):
        slot = block_slot(n)
        sib_in(n, slot).wait_recv()
        scaled = []
        for cs in range(2):
            a = abuf[cs, slot]
            wide = a.astype(F32)
            ssq[...] += wide[:, :128] * wide[:, :128] + wide[:, 128:] * wide[:, 128:]
            scaled.append(a * gain_row(cs * NZ + slot).astype(BF16))
        acc[c, 0:256, :] += lax.dot_general(
            jnp.concatenate([ubuf[slot], ubuf[NZ + slot]], axis=0), jnp.concatenate(scaled, axis=1),
            (((0,), (1,)), ((), ())), preferred_element_type=F32)
        return carry

    def loop_step(i, carry):
        ring_step(i, 2)

        @pl.when(jnp.logical_not(mine))
        def _():
            for k in range(2):
                u_direct_in(2 * (i - 1) + k).wait_recv()
                u_mate(2 * (i - 1) + k).start()
        return carry

    lax.fori_loop(1, 5, loop_step, 0)
    ring_step(5, 2)

    @pl.when(jnp.logical_not(mine))
    def _():
        def wait_u(k, carry):
            u_mate_in(k).wait_recv()
            return carry

        lax.fori_loop(0, 8, wait_u, 0)

    @pl.when(mine)
    def _():
        u_local.wait()

    lax.fori_loop(0, 5, blocks, 0)
    ring_step(6, 2)
    lax.fori_loop(5, 10, blocks, 0)
    ring_step(7, 1)
    lax.fori_loop(10, 15, blocks, 0)
    for d in range(2):
        ring_in(d, d, 8).wait_recv()
    sib(15, (z + 8) % NZ).start()
    blocks(15, 0)

    def gather_done():
        def ring_done(i, carry):
            for h in range(2):
                for d in range(2):
                    ring(d, h, i).wait_send()
            return carry

        lax.fori_loop(1, 8, ring_done, 0)
        for d in range(2):
            ring(d, d, 8).wait_send()

        def sib_done(n, carry):
            sib(n, block_slot(n)).wait_send()
            return carry

        lax.fori_loop(0, 16, sib_done, 0)

        @pl.when(mine)
        def _():
            def done(k, carry):
                u_direct(k).wait_send()
                return carry

            lax.fori_loop(0, 8, done, 0)

        @pl.when(jnp.logical_not(mine))
        def _():
            for h in range(2):
                swap(h).wait_send()

            def done(k, carry):
                u_mate(k).wait_send()
                return carry

            lax.fori_loop(0, 8, done, 0)

    t_copy.wait_recv()
    t2x = jnp.where(mine, tsrc[0:2, :], tbuf[0:2, :])
    tgt = jnp.concatenate([t2x[0:1, :], t2x[1:2, :], t2x[0:1, :], t2x[1:2, :]], axis=1)
    scale_row = jnp.where(lax.broadcasted_iota(jnp.int32, (1, 512), 1) < 256, scale_ref[0], scale_ref[1])
    mean_sq = jnp.sum(ssq[...].T, axis=0, keepdims=True) * (1.0 / 8192.0)
    r_row = lax.rsqrt(mean_sq + norm_eps)

    def as_tile(row):
        return [row[:, 128 * k:128 * k + 128] for k in range(4)]

    def lane_sum(row):
        return row[:, :128] + row[:, 128:256] + row[:, 256:384] + row[:, 384:]

    def is_target(plane):
        return lax.broadcasted_iota(jnp.int32, (256, 512), 0).astype(F32) == tgt - ((plane * NZ + z) * 256).astype(F32)

    logits = acc[c, 0:256, :] * r_row
    m = jnp.max(logits, axis=0, keepdims=True)
    ex = jnp.exp(logits - m)
    acc[c, 0:256, :] = ex
    acc[c, 256:264, :] = jnp.broadcast_to(m, (8, 512))
    part_lse = m + jnp.log(jnp.sum(ex, axis=0, keepdims=True))
    part_t = lane_sum(jnp.sum(jnp.where(is_target(c), logits, 0.0), axis=0, keepdims=True) * scale_row)
    zst[z] = jnp.concatenate(as_tile(part_lse) + [part_t] * 4, axis=0)

    def z_copy(k):
        return rcopy(zst.at[z], zst.at[z], z_s.at[k], z_r.at[k], dev(x, y, (z + k) % NZ, c))

    def z_in(k):
        slot = (z + NZ - k) % NZ
        return rcopy(zst.at[slot], zst.at[slot], z_s.at[k], z_r.at[k], dev(x, y, (z + k) % NZ, c))

    def z_all(act):
        def body(k, carry):
            act(k)
            return carry

        lax.fori_loop(1, NZ, body, 0)

    for k in range(1, NZ):
        z_copy(k).start()
    lg_copy = rcopy(acc.at[c], acc.at[c], lg_sem.at[0], lg_sem.at[1], sibling)
    lg_in = rcopy(acc.at[1 - c], acc.at[1 - c], lg_sem.at[0], lg_sem.at[1], sibling)
    lg_copy.start()
    gather_done()
    weight = scale_row * r_row
    z_all(lambda k: z_in(k).wait_recv())

    st = zst[...]
    l16 = st[:, 0:4, :]
    top = jnp.max(l16, axis=0)
    plane_lse = top + jnp.log(jnp.sum(jnp.exp(l16 - top[None]), axis=0))
    lebuf[c] = jnp.concatenate([plane_lse, jnp.sum(st[:, 4:8, :], axis=0)], axis=0)
    le_copy = rcopy(lebuf.at[c], lebuf.at[c], le_sem.at[0], le_sem.at[1], sibling)
    le_in = rcopy(lebuf.at[1 - c], lebuf.at[1 - c], le_sem.at[0], le_sem.at[1], sibling)
    le_copy.start()
    lg_in.wait_recv()
    le_in.wait_recv()
    l_a, l_b = lebuf[0, 0:4, :], lebuf[1, 0:4, :]
    l_top = jnp.maximum(l_a, l_b)
    lse = l_top + jnp.log(jnp.exp(l_a - l_top) + jnp.exp(l_b - l_top))
    lse_row = jnp.concatenate([lse[k:k + 1, :] for k in range(4)], axis=1)

    def gradient(plane):
        share = jnp.exp(acc[plane, 256:257, :] - lse_row)
        gbuf[plane] = (weight * (acc[plane, 0:256, :] * share - is_target(plane).astype(F32))).astype(BF16)

    def l_copy(axis, k):
        if axis == 0:
            return rcopy(lx.at[x], lx.at[x], l_s.at[0, k], l_r.at[0, k], dev((x + k) % 4, y, z, c))
        return rcopy(ly.at[y], ly.at[y], l_s.at[1, k], l_r.at[1, k], dev(x, (y + k) % 4, z, c))

    def l_in(axis, k):
        if axis == 0:
            slot = (x + 4 - k) % 4
            return rcopy(lx.at[slot], lx.at[slot], l_s.at[0, k], l_r.at[0, k], dev((x + k) % 4, y, z, c))
        slot = (y + 4 - k) % 4
        return rcopy(ly.at[slot], ly.at[slot], l_s.at[1, k], l_r.at[1, k], dev(x, (y + k) % 4, z, c))

    def loss_x():
        lx[x] = jnp.broadcast_to(lane_sum(scale_row * lse_row), (8, 128)) - (
            jnp.broadcast_to(lebuf[0, 4:5, :], (8, 128)) + jnp.broadcast_to(lebuf[1, 4:5, :], (8, 128)))
        for k in range(1, 4):
            l_copy(0, k).start()

    def loss_y():
        for k in range(1, 4):
            l_in(0, k).wait_recv()
        ly[y] = lx[0] + lx[1] + lx[2] + lx[3]
        for k in range(1, 4):
            l_copy(1, k).start()

    def loss_end():
        for k in range(1, 4):
            l_in(1, k).wait_recv()
        tot = ly[0] + ly[1] + ly[2] + ly[3]
        loss_ref[0] = jnp.sum(tot[0:1, :]) * (1.0 / 4096.0)

    def along(axis, step):
        if axis == 0:
            return dev((x + step) % 4, y, z, c)
        return dev(x, (y + step) % 4, z, c)

    def grad_block(dy, dx):
        y_, x_ = (y + dy) % 4, (x + dx) % 4
        s = ((y_ * 2 + x_ % 2) * 2 + c) * 2
        plane, slot = s // NZ, s % NZ
        for k in range(2):
            pbuf[y_, x_, :, 256 * k:256 * k + 256] = jnp.dot(
                gbuf[x_ // 2], abuf[plane, slot + k], preferred_element_type=F32).astype(BF16)

    def blk(axis, step, o):
        if axis == 0:
            return pbuf.at[(y + o) % 4, (x + step) % 4]
        return pbuf.at[(y + step) % 4, (x + o) % 4]

    def part(axis, which):
        return pl.ds(128 * axis + 64 * which, 64)

    STEP = (1, 3)

    def send_o(axis, d, o):
        return rcopy(blk(axis, 2, o).at[part(axis, d)], r_o.at[axis, d, o], rs_s.at[0, axis, d, o], rs_r.at[0, axis, d, o], along(axis, STEP[d]))

    def send_d(axis, d, o):
        return rcopy(blk(axis, STEP[d], o).at[part(axis, 1 - d)], r_d.at[axis, d, o], rs_s.at[1, axis, d, o], rs_r.at[1, axis, d, o], along(axis, STEP[d]))

    def send_c(axis, d, o):
        return rcopy(blk(axis, STEP[d], o).at[part(axis, d)], r_c.at[axis, d, o], rs_s.at[2, axis, d, o], rs_r.at[2, axis, d, o], along(axis, STEP[d]))

    def send_o2(axis, d):
        return rcopy(blk(axis, 0, 2).at[part(axis, d)], q_o.at[axis, d], qs_s.at[0, axis, d], qs_r.at[0, axis, d], along(1 - axis, STEP[d]))

    def send_d2(axis, d):
        return rcopy(blk(axis, 0, STEP[d]).at[part(axis, 1 - d)], q_d.at[axis, d], qs_s.at[1, axis, d], qs_r.at[1, axis, d], along(1 - axis, STEP[d]))

    def send_c2(axis, d):
        return rcopy(blk(axis, 0, STEP[d]).at[part(axis, d)], q_c.at[axis, d], qs_s.at[2, axis, d], qs_r.at[2, axis, d], along(1 - axis, STEP[d]))

    def start_o(axis, o):
        for d in range(2):
            send_o(axis, d, o).start()

    def start_d(axis, o):
        for d in range(2):
            send_d(axis, d, o).start()

    def pair_sum(axis, d, o):
        send_o(axis, d, o).wait_recv()
        ref = blk(axis, STEP[d], o)
        rows = part(axis, d)
        ref[rows, :] = ref[rows, :] + r_o[axis, d, o]
        send_c(axis, d, o).start()

    def pair_sums(o):
        for axis in range(2):
            for d in range(2):
                pair_sum(axis, d, o)

    def first_pass(o):
        for axis in range(2):
            own = blk(axis, 0, o)
            for w in range(2):
                send_c(axis, w, o).wait_recv()
                send_d(axis, 1 - w, o).wait_recv()
                rows = part(axis, w)
                total = own[rows, :].astype(F32) + r_c[axis, w, o].astype(F32) + r_d[axis, 1 - w, o].astype(F32)
                if o == 0:
                    fin[rows, :] = total
                else:
                    own[rows, :] = total.astype(BF16)
                if o == 2:
                    send_o2(axis, w).start()
            if o in STEP:
                send_d2(axis, STEP.index(o)).start()

    def both(start, o):
        for axis in range(2):
            start(axis, o)

    gradient(1 - xh)
    grad_block(2, 2)
    both(start_o, 2)
    for o in (1, 3, 0):
        grad_block(o, 2)
        start_o(0, o)
    gradient(xh)
    for o in (1, 3, 0):
        grad_block(2, o)
        start_o(1, o)
    pair_sums(2)
    both(start_d, 2)
    loss_x()
    for dy in (1, 3):
        for dx in (1, 3):
            grad_block(dy, dx)
    both(start_d, 1)
    both(start_d, 3)
    pair_sums(1)
    pair_sums(3)
    first_pass(2)
    for k in (1, 3):
        grad_block(0, k)
        grad_block(k, 0)
    both(start_d, 0)
    pair_sums(0)
    loss_y()
    first_pass(1)
    first_pass(3)
    grad_block(0, 0)
    for axis in range(2):
        for d in range(2):
            send_o2(axis, d).wait_recv()
            ref = blk(axis, 0, STEP[d])
            rows = part(axis, d)
            ref[rows, :] = ref[rows, :] + q_o[axis, d]
            send_c2(axis, d).start()
    first_pass(0)
    loss_end()

    for axis in range(2):
        for d in range(2):
            for o in range(4):
                send_o(axis, d, o).wait_send()
                send_d(axis, d, o).wait_send()
                send_c(axis, d, o).wait_send()
        for k in range(1, 4):
            l_copy(axis, k).wait_send()
    for copy in (t_copy, lg_copy, le_copy):
        copy.wait_send()
    z_all(lambda k: z_copy(k).wait_send())

    s_own = ((y * 2 + xl) * 2 + c) * 2
    gain_own = jnp.concatenate([gain_row(s_own), gain_row(s_own + 1)], axis=1)
    for axis in range(2):
        for w in range(2):
            send_c2(axis, w).wait_recv()
            send_d2(axis, 1 - w).wait_recv()
            rows = part(axis, w)
            fin[rows, :] = (fin[rows, :] + q_c[axis, w].astype(F32) + q_d[axis, 1 - w].astype(F32)) * gain_own
        o_ref[:, 128 * axis:128 * axis + 128] = fin[pl.ds(128 * axis, 128), :].T

    for axis in range(2):
        for d in range(2):
            send_o2(axis, d).wait_send()
            send_d2(axis, d).wait_send()
            send_c2(axis, d).wait_send()


def per_device(hidden_states, exit_layers, targets, norm_gain, exit_scale, unembedding):
    vmem = pl.BlockSpec(memory_space=pltpu.VMEM)
    smem = pl.BlockSpec(memory_space=pltpu.SMEM)
    anywhere = pl.BlockSpec(memory_space=pltpu.HBM)
    dma = pltpu.SemaphoreType.DMA
    grad, loss = pl.pallas_call(
        kernel,
        out_shape=(jax.ShapeDtypeStruct((512, 256), F32), jax.ShapeDtypeStruct((1,), F32)),
        in_specs=[anywhere] * 6,
        out_specs=(vmem, smem),
        scratch_shapes=[
            pltpu.SMEM((2, 4), jnp.int32), pltpu.SMEM((2,), F32), pltpu.VMEM((2, 128), jnp.int32),
            pltpu.VMEM((64, 128), BF16),
            pltpu.VMEM((4, 256, 256), BF16),
            pltpu.VMEM((512, 256), BF16),
            pltpu.VMEM((8, 128), F32),
            pltpu.VMEM((64, 128), F32),
            dma((5,)),
            pltpu.VMEM((2, 16, 512, 256), BF16),
            pltpu.VMEM((32, 256, 256), BF16),
            pltpu.VMEM((2, 264, 512), F32),
            pltpu.VMEM((512, 128), F32),
            pltpu.VMEM((2, 256, 512), BF16),
            pltpu.VMEM((8, 128), F32),
            pltpu.VMEM((16, 8, 128), F32),
            pltpu.VMEM((2, 8, 128), F32),
            pltpu.VMEM((4, 8, 128), F32),
            pltpu.VMEM((4, 8, 128), F32),
            pltpu.VMEM((4, 4, 256, 512), BF16),
            pltpu.VMEM((256, 512), F32),
            pltpu.VMEM((2, 2, 4, 64, 512), BF16),
            pltpu.VMEM((2, 2, 4, 64, 512), BF16),
            pltpu.VMEM((2, 2, 4, 64, 512), BF16),
            pltpu.VMEM((2, 2, 64, 512), BF16),
            pltpu.VMEM((2, 2, 64, 512), BF16),
            pltpu.VMEM((2, 2, 64, 512), BF16),
            dma((2, 2)), dma((2, 2, 8)), dma((2, 2, 8)), dma((16,)), dma((16,)),
            dma((2, 8)), dma((2, 8)), dma, dma((2,)), dma((2,)), dma((16,)), dma((16,)), dma((2,)),
            dma((2, 4)), dma((2, 4)), dma((3, 2, 2, 4)), dma((3, 2, 2, 4)), dma((3, 2, 2)), dma((3, 2, 2)),
        ],
        compiler_params=pltpu.CompilerParams(
            collective_id=0, has_side_effects=True, vmem_limit_bytes=30 << 20),
    )(*[pltpu.with_memory_space_constraint(a, pltpu.HBM) for a in (
        exit_layers.T, exit_scale, hidden_states, unembedding.reshape(32, 256, 256),
        targets.reshape(2, 128), norm_gain.reshape(64, 128))])
    return (grad, loss.reshape(()))


def solution(mesh):
    in_specs = (P(None, "dp", "vocab"), P("dp", None), P("dp"), P(), P(), P(None, "vocab"))
    out_specs = (P("dp", "vocab"), P())
    return jax.shard_map(
        per_device, mesh=mesh, in_specs=in_specs, out_specs=out_specs, check_vma=False
    )
```

```python
import jax
import jax.numpy as jnp
from jax import lax
from jax.experimental import pallas as pl
from jax.experimental.pallas import tpu as pltpu
from jax.sharding import PartitionSpec as P

norm_eps = 1e-05
MESH = pl.DeviceIdType.MESH
F32 = jnp.float32
BF16 = jnp.bfloat16
NZ, NX, NY = 16, 4, 4


def kernel(el_any, scale_any, hid_ref, u_ref, tgt_any, gain_any, o_ref, loss_ref,
           el_ref, scale_ref, tgt_ref, gain_ref, hbuf, xbuf, tsrc, gain, in_sem,
           abuf, ubuf, acc, ssq, gbuf, tbuf, zst, lebuf, lx, ly, pbuf, fin,
           r_o, r_d, r_c, q_o, q_d, q_c,
           swap_sem, ring_s, ring_r, sib_s, sib_r, u_s, u_r, u_loc, t_sem, lg_sem, z_s, z_r, le_sem,
           l_s, l_r, rs_s, rs_r, qs_s, qs_r):
    dp = lax.axis_index("dp")
    vo = lax.axis_index("vocab")
    c = dp % 2
    xl = (dp // 2) % 2
    y = dp // 4
    z = vo % NZ
    xh = vo // NZ
    x = xh * 2 + xl

    def dev(x_, y_, z_, c_):
        return ((y_ * 2 + x_ % 2) * 2 + c_, (x_ // 2) * NZ + z_)

    sibling = dev(x, y, z, 1 - c)
    partner = dev((x + 2) % 4, y, z, 1 - c)

    def rcopy(src, dst, s, r, to):
        return pltpu.make_async_remote_copy(src_ref=src, dst_ref=dst, send_sem=s, recv_sem=r,
                                            device_id=to, device_id_type=MESH)

    inputs = [pltpu.make_async_copy(a, b, in_sem.at[k]) for k, (a, b) in enumerate((
        (hid_ref, hbuf), (el_any, el_ref), (scale_any, scale_ref), (tgt_any, tgt_ref), (gain_any, gain_ref)))]
    for copy in inputs[:2]:
        copy.start()

    bar = pltpu.get_barrier_semaphore()
    for to in (sibling, partner, dev(x, y, (z + 1) % NZ, c), dev(x, y, (z + NZ - 1) % NZ, c)):
        pl.semaphore_signal(bar, inc=1, device_id=to, device_id_type=MESH)
    for k in range(1, 4):
        pl.semaphore_signal(bar, inc=1, device_id=dev((x + k) % 4, y, z, c), device_id_type=MESH)
        pl.semaphore_signal(bar, inc=1, device_id=dev(x, (y + k) % 4, z, c), device_id_type=MESH)

    for copy in inputs[2:]:
        copy.start()

    def select(dst):
        for e in range(2):
            for row in range(4):
                dst[pl.ds(256 * e + 64 * row, 64), :] = hbuf[el_ref[e, row], pl.ds(64 * row, 64), :]

    mine = c == xh
    for copy in inputs[:2]:
        copy.wait()

    @pl.when(mine)
    def _():
        select(abuf.at[c, z])

    @pl.when(jnp.logical_not(mine))
    def _():
        select(xbuf)

    pl.semaphore_wait(bar, 10)

    def swap(h):
        rows = pl.ds(256 * h, 256)
        return rcopy(xbuf.at[rows], abuf.at[1 - c, z, rows], swap_sem.at[0, h], swap_sem.at[1, h], partner)

    def swap_in(h):
        ref = abuf.at[c, z, pl.ds(256 * h, 256)]
        return rcopy(ref, ref, swap_sem.at[0, h], swap_sem.at[1, h], partner)

    def u_direct(k):
        j = (1 - xl) * 8 + k
        return rcopy(u_ref.at[pl.ds(2 * j, 2)], ubuf.at[pl.ds(2 * j, 2)], u_s.at[0, k], u_r.at[0, k], dev(3 - x, y, z, c))

    def u_direct_in(k):
        j = xl * 8 + k
        return rcopy(ubuf.at[pl.ds(2 * j, 2)], ubuf.at[pl.ds(2 * j, 2)], u_s.at[0, k], u_r.at[0, k], dev(3 - x, y, z, c))

    def u_mate(k):
        j = xl * 8 + k
        return rcopy(ubuf.at[pl.ds(2 * j, 2)], ubuf.at[pl.ds(2 * j, 2)], u_s.at[1, k], u_r.at[1, k], dev(xh * 2 + 1 - xl, y, z, c))

    def u_mate_in(k):
        j = (1 - xl) * 8 + k
        return rcopy(ubuf.at[pl.ds(2 * j, 2)], ubuf.at[pl.ds(2 * j, 2)], u_s.at[1, k], u_r.at[1, k], dev(xh * 2 + 1 - xl, y, z, c))

    u_local = pltpu.make_async_copy(u_ref, ubuf, u_loc)

    @pl.when(jnp.logical_not(mine))
    def _():
        for h in range(2):
            swap(h).start()

    def step_slot(d, i):
        return (z - i + NZ) % NZ if d == 0 else (z + i) % NZ

    def half(slot, h):
        return abuf.at[c, slot, pl.ds(256 * h, 256)]

    def ring(d, h, i):
        ref = half(step_slot(d, i - 1), h)
        to = dev(x, y, (z + 1) % NZ, c) if d == 0 else dev(x, y, (z + NZ - 1) % NZ, c)
        return rcopy(ref, ref, ring_s.at[d, h, i - 1], ring_r.at[d, h, i - 1], to)

    def ring_in(d, h, i):
        ref = half(step_slot(d, i), h)
        to = dev(x, y, (z + 1) % NZ, c) if d == 0 else dev(x, y, (z + NZ - 1) % NZ, c)
        return rcopy(ref, ref, ring_s.at[d, h, i - 1], ring_r.at[d, h, i - 1], to)

    def sib(n, slot):
        ref = abuf.at[c, slot]
        return rcopy(ref, ref, sib_s.at[n], sib_r.at[n], sibling)

    def sib_in(n, slot):
        ref = abuf.at[1 - c, slot]
        return rcopy(ref, ref, sib_s.at[n], sib_r.at[n], sibling)

    for h in range(2):
        @pl.when(jnp.logical_not(mine))
        def _():
            swap_in(h).wait_recv()

        for d in range(2):
            ring(d, h, 1).start()
    sib(0, z).start()

    for copy in inputs[2:]:
        copy.wait()
    tsrc[0:2, :] = tgt_ref[...].astype(F32)
    t_copy = rcopy(tsrc, tbuf, t_sem.at[0], t_sem.at[1], sibling)
    t_copy.start()

    @pl.when(mine)
    def _():
        def send_u(k, carry):
            u_direct(k).start()
            return carry

        lax.fori_loop(0, 8, send_u, 0)
        u_local.start()


    gain[...] = gain_ref[...].astype(F32)

    def gain_row(s):
        return jnp.concatenate([gain[pl.ds(2 * s, 1), :], gain[pl.ds(2 * s + 1, 1), :]], axis=1)

    acc[c, 0:256, :] = jnp.zeros((256, 512), F32)
    ssq[...] = jnp.zeros_like(ssq)

    def ring_step(i, more):
        for h in range(2):
            for d in range(2):
                ring_in(d, h, i).wait_recv()
                if more == 2 or (more == 1 and h == d):
                    ring(d, h, i + 1).start()
        for d in range(2):
            sib(2 * i - d, step_slot(d, i)).start()

    def block_slot(n):
        off = jnp.where(n % 2 == 1, (n + 1) // 2, NZ - n // 2)
        return (z + off) % NZ

    def blocks(n, carry):
        slot = block_slot(n)
        sib_in(n, slot).wait_recv()
        scaled = []
        for cs in range(2):
            a = abuf[cs, slot]
            wide = a.astype(F32)
            ssq[...] += wide[:, :128] * wide[:, :128] + wide[:, 128:] * wide[:, 128:]
            scaled.append(a * gain_row(cs * NZ + slot).astype(BF16))
        acc[c, 0:256, :] += lax.dot_general(
            jnp.concatenate([ubuf[slot], ubuf[NZ + slot]], axis=0), jnp.concatenate(scaled, axis=1),
            (((0,), (1,)), ((), ())), preferred_element_type=F32)
        return carry

    def loop_step(i, carry):
        ring_step(i, 2)

        @pl.when(jnp.logical_not(mine))
        def _():
            for k in range(2):
                u_direct_in(2 * (i - 1) + k).wait_recv()
                u_mate(2 * (i - 1) + k).start()
        return carry

    lax.fori_loop(1, 5, loop_step, 0)
    ring_step(5, 2)

    @pl.when(jnp.logical_not(mine))
    def _():
        def wait_u(k, carry):
            u_mate_in(k).wait_recv()
            return carry

        lax.fori_loop(0, 8, wait_u, 0)

    @pl.when(mine)
    def _():
        u_local.wait()

    lax.fori_loop(0, 5, blocks, 0)
    ring_step(6, 2)
    lax.fori_loop(5, 10, blocks, 0)
    ring_step(7, 1)
    lax.fori_loop(10, 15, blocks, 0)
    for d in range(2):
        ring_in(d, d, 8).wait_recv()
    sib(15, (z + 8) % NZ).start()
    blocks(15, 0)

    def gather_done():
        def ring_done(i, carry):
            for h in range(2):
                for d in range(2):
                    ring(d, h, i).wait_send()
            return carry

        lax.fori_loop(1, 8, ring_done, 0)
        for d in range(2):
            ring(d, d, 8).wait_send()

        def sib_done(n, carry):
            sib(n, block_slot(n)).wait_send()
            return carry

        lax.fori_loop(0, 16, sib_done, 0)

        @pl.when(mine)
        def _():
            def done(k, carry):
                u_direct(k).wait_send()
                return carry

            lax.fori_loop(0, 8, done, 0)

        @pl.when(jnp.logical_not(mine))
        def _():
            for h in range(2):
                swap(h).wait_send()

            def done(k, carry):
                u_mate(k).wait_send()
                return carry

            lax.fori_loop(0, 8, done, 0)

    t_copy.wait_recv()
    t2x = jnp.where(mine, tsrc[0:2, :], tbuf[0:2, :])
    tgt = jnp.concatenate([t2x[0:1, :], t2x[1:2, :], t2x[0:1, :], t2x[1:2, :]], axis=1)
    scale_row = jnp.where(lax.broadcasted_iota(jnp.int32, (1, 512), 1) < 256, scale_ref[0], scale_ref[1])
    mean_sq = jnp.sum(ssq[...].T, axis=0, keepdims=True) * (1.0 / 8192.0)
    r_row = lax.rsqrt(mean_sq + norm_eps)

    def as_tile(row):
        return [row[:, 128 * k:128 * k + 128] for k in range(4)]

    def lane_sum(row):
        return row[:, :128] + row[:, 128:256] + row[:, 256:384] + row[:, 384:]

    def is_target(plane):
        return lax.broadcasted_iota(jnp.int32, (256, 512), 0).astype(F32) == tgt - ((plane * NZ + z) * 256).astype(F32)

    logits = acc[c, 0:256, :] * r_row
    m = jnp.max(logits, axis=0, keepdims=True)
    ex = jnp.exp(logits - m)
    acc[c, 0:256, :] = ex
    acc[c, 256:264, :] = jnp.broadcast_to(m, (8, 512))
    part_lse = m + jnp.log(jnp.sum(ex, axis=0, keepdims=True))
    part_t = lane_sum(jnp.sum(jnp.where(is_target(c), logits, 0.0), axis=0, keepdims=True) * scale_row)
    zst[z] = jnp.concatenate(as_tile(part_lse) + [part_t] * 4, axis=0)

    def z_copy(k):
        return rcopy(zst.at[z], zst.at[z], z_s.at[k], z_r.at[k], dev(x, y, (z + k) % NZ, c))

    def z_in(k):
        slot = (z + NZ - k) % NZ
        return rcopy(zst.at[slot], zst.at[slot], z_s.at[k], z_r.at[k], dev(x, y, (z + k) % NZ, c))

    def z_all(act):
        def body(k, carry):
            act(k)
            return carry

        lax.fori_loop(1, NZ, body, 0)

    for k in range(1, NZ):
        z_copy(k).start()
    lg_copy = rcopy(acc.at[c], acc.at[c], lg_sem.at[0], lg_sem.at[1], sibling)
    lg_in = rcopy(acc.at[1 - c], acc.at[1 - c], lg_sem.at[0], lg_sem.at[1], sibling)
    lg_copy.start()
    gather_done()
    weight = scale_row * r_row
    z_all(lambda k: z_in(k).wait_recv())

    st = zst[...]
    l16 = st[:, 0:4, :]
    top = jnp.max(l16, axis=0)
    plane_lse = top + jnp.log(jnp.sum(jnp.exp(l16 - top[None]), axis=0))
    lebuf[c] = jnp.concatenate([plane_lse, jnp.sum(st[:, 4:8, :], axis=0)], axis=0)
    le_copy = rcopy(lebuf.at[c], lebuf.at[c], le_sem.at[0], le_sem.at[1], sibling)
    le_in = rcopy(lebuf.at[1 - c], lebuf.at[1 - c], le_sem.at[0], le_sem.at[1], sibling)
    le_copy.start()
    lg_in.wait_recv()
    le_in.wait_recv()
    l_a, l_b = lebuf[0, 0:4, :], lebuf[1, 0:4, :]
    l_top = jnp.maximum(l_a, l_b)
    lse = l_top + jnp.log(jnp.exp(l_a - l_top) + jnp.exp(l_b - l_top))
    lse_row = jnp.concatenate([lse[k:k + 1, :] for k in range(4)], axis=1)

    def gradient(plane):
        share = jnp.exp(acc[plane, 256:257, :] - lse_row)
        gbuf[plane] = (weight * (acc[plane, 0:256, :] * share - is_target(plane).astype(F32))).astype(BF16)

    def l_copy(axis, k):
        if axis == 0:
            return rcopy(lx.at[x], lx.at[x], l_s.at[0, k], l_r.at[0, k], dev((x + k) % 4, y, z, c))
        return rcopy(ly.at[y], ly.at[y], l_s.at[1, k], l_r.at[1, k], dev(x, (y + k) % 4, z, c))

    def l_in(axis, k):
        if axis == 0:
            slot = (x + 4 - k) % 4
            return rcopy(lx.at[slot], lx.at[slot], l_s.at[0, k], l_r.at[0, k], dev((x + k) % 4, y, z, c))
        slot = (y + 4 - k) % 4
        return rcopy(ly.at[slot], ly.at[slot], l_s.at[1, k], l_r.at[1, k], dev(x, (y + k) % 4, z, c))

    def loss_x():
        lx[x] = jnp.broadcast_to(lane_sum(scale_row * lse_row), (8, 128)) - (
            jnp.broadcast_to(lebuf[0, 4:5, :], (8, 128)) + jnp.broadcast_to(lebuf[1, 4:5, :], (8, 128)))
        for k in range(1, 4):
            l_copy(0, k).start()

    def loss_y():
        for k in range(1, 4):
            l_in(0, k).wait_recv()
        ly[y] = lx[0] + lx[1] + lx[2] + lx[3]
        for k in range(1, 4):
            l_copy(1, k).start()

    def loss_end():
        for k in range(1, 4):
            l_in(1, k).wait_recv()
        tot = ly[0] + ly[1] + ly[2] + ly[3]
        loss_ref[0] = jnp.sum(tot[0:1, :]) * (1.0 / 4096.0)

    def along(axis, step):
        if axis == 0:
            return dev((x + step) % 4, y, z, c)
        return dev(x, (y + step) % 4, z, c)

    def grad_block(dy, dx):
        y_, x_ = (y + dy) % 4, (x + dx) % 4
        s = ((y_ * 2 + x_ % 2) * 2 + c) * 2
        plane, slot = s // NZ, s % NZ
        for k in range(2):
            pbuf[y_, x_, :, 256 * k:256 * k + 256] = jnp.dot(
                gbuf[x_ // 2], abuf[plane, slot + k], preferred_element_type=F32).astype(BF16)

    def blk(axis, step, o):
        if axis == 0:
            return pbuf.at[(y + o) % 4, (x + step) % 4]
        return pbuf.at[(y + step) % 4, (x + o) % 4]

    def part(axis, which):
        return pl.ds(128 * axis + 64 * which, 64)

    STEP = (1, 3)

    def send_o(axis, d, o):
        return rcopy(blk(axis, 2, o).at[part(axis, d)], r_o.at[axis, d, o], rs_s.at[0, axis, d, o], rs_r.at[0, axis, d, o], along(axis, STEP[d]))

    def send_d(axis, d, o):
        return rcopy(blk(axis, STEP[d], o).at[part(axis, 1 - d)], r_d.at[axis, d, o], rs_s.at[1, axis, d, o], rs_r.at[1, axis, d, o], along(axis, STEP[d]))

    def send_c(axis, d, o):
        return rcopy(blk(axis, STEP[d], o).at[part(axis, d)], r_c.at[axis, d, o], rs_s.at[2, axis, d, o], rs_r.at[2, axis, d, o], along(axis, STEP[d]))

    def send_o2(axis, d):
        return rcopy(blk(axis, 0, 2).at[part(axis, d)], q_o.at[axis, d], qs_s.at[0, axis, d], qs_r.at[0, axis, d], along(1 - axis, STEP[d]))

    def send_d2(axis, d):
        return rcopy(blk(axis, 0, STEP[d]).at[part(axis, 1 - d)], q_d.at[axis, d], qs_s.at[1, axis, d], qs_r.at[1, axis, d], along(1 - axis, STEP[d]))

    def send_c2(axis, d):
        return rcopy(blk(axis, 0, STEP[d]).at[part(axis, d)], q_c.at[axis, d], qs_s.at[2, axis, d], qs_r.at[2, axis, d], along(1 - axis, STEP[d]))

    def start_o(axis, o):
        for d in range(2):
            send_o(axis, d, o).start()

    def start_d(axis, o):
        for d in range(2):
            send_d(axis, d, o).start()

    def pair_sum(axis, d, o):
        send_o(axis, d, o).wait_recv()
        ref = blk(axis, STEP[d], o)
        rows = part(axis, d)
        ref[rows, :] = ref[rows, :] + r_o[axis, d, o]
        send_c(axis, d, o).start()

    def pair_sums(o):
        for axis in range(2):
            for d in range(2):
                pair_sum(axis, d, o)

    def first_pass(o):
        for axis in range(2):
            own = blk(axis, 0, o)
            for w in range(2):
                send_c(axis, w, o).wait_recv()
                send_d(axis, 1 - w, o).wait_recv()
                rows = part(axis, w)
                total = own[rows, :].astype(F32) + r_c[axis, w, o].astype(F32) + r_d[axis, 1 - w, o].astype(F32)
                if o == 0:
                    fin[rows, :] = total
                else:
                    own[rows, :] = total.astype(BF16)
                if o == 2:
                    send_o2(axis, w).start()
            if o in STEP:
                send_d2(axis, STEP.index(o)).start()

    def both(start, o):
        for axis in range(2):
            start(axis, o)

    gradient(1 - xh)
    grad_block(2, 2)
    both(start_o, 2)
    for o in (1, 3, 0):
        grad_block(o, 2)
        start_o(0, o)
    gradient(xh)
    for o in (1, 3, 0):
        grad_block(2, o)
        start_o(1, o)
    pair_sums(2)
    both(start_d, 2)
    loss_x()
    for dy in (1, 3):
        for dx in (1, 3):
            grad_block(dy, dx)
    pair_sums(1)
    both(start_d, 1)
    pair_sums(3)
    both(start_d, 3)
    first_pass(2)
    for k in (1, 3):
        grad_block(0, k)
        grad_block(k, 0)
    pair_sums(0)
    both(start_d, 0)
    loss_y()
    first_pass(1)
    first_pass(3)
    grad_block(0, 0)
    for axis in range(2):
        for d in range(2):
            send_o2(axis, d).wait_recv()
            ref = blk(axis, 0, STEP[d])
            rows = part(axis, d)
            ref[rows, :] = ref[rows, :] + q_o[axis, d]
            send_c2(axis, d).start()
    first_pass(0)
    loss_end()

    for axis in range(2):
        for d in range(2):
            for o in range(4):
                send_o(axis, d, o).wait_send()
                send_d(axis, d, o).wait_send()
                send_c(axis, d, o).wait_send()
        for k in range(1, 4):
            l_copy(axis, k).wait_send()
    for copy in (t_copy, lg_copy, le_copy):
        copy.wait_send()
    z_all(lambda k: z_copy(k).wait_send())

    s_own = ((y * 2 + xl) * 2 + c) * 2
    gain_own = jnp.concatenate([gain_row(s_own), gain_row(s_own + 1)], axis=1)
    for axis in range(2):
        for w in range(2):
            send_c2(axis, w).wait_recv()
            send_d2(axis, 1 - w).wait_recv()
            rows = part(axis, w)
            fin[rows, :] = (fin[rows, :] + q_c[axis, w].astype(F32) + q_d[axis, 1 - w].astype(F32)) * gain_own
        o_ref[:, 128 * axis:128 * axis + 128] = fin[pl.ds(128 * axis, 128), :].T

    for axis in range(2):
        for d in range(2):
            send_o2(axis, d).wait_send()
            send_d2(axis, d).wait_send()
            send_c2(axis, d).wait_send()


def per_device(hidden_states, exit_layers, targets, norm_gain, exit_scale, unembedding):
    vmem = pl.BlockSpec(memory_space=pltpu.VMEM)
    smem = pl.BlockSpec(memory_space=pltpu.SMEM)
    anywhere = pl.BlockSpec(memory_space=pltpu.HBM)
    dma = pltpu.SemaphoreType.DMA
    grad, loss = pl.pallas_call(
        kernel,
        out_shape=(jax.ShapeDtypeStruct((512, 256), F32), jax.ShapeDtypeStruct((1,), F32)),
        in_specs=[anywhere] * 6,
        out_specs=(vmem, smem),
        scratch_shapes=[
            pltpu.SMEM((2, 4), jnp.int32), pltpu.SMEM((2,), F32), pltpu.VMEM((2, 128), jnp.int32),
            pltpu.VMEM((64, 128), BF16),
            pltpu.VMEM((4, 256, 256), BF16),
            pltpu.VMEM((512, 256), BF16),
            pltpu.VMEM((8, 128), F32),
            pltpu.VMEM((64, 128), F32),
            dma((5,)),
            pltpu.VMEM((2, 16, 512, 256), BF16),
            pltpu.VMEM((32, 256, 256), BF16),
            pltpu.VMEM((2, 264, 512), F32),
            pltpu.VMEM((512, 128), F32),
            pltpu.VMEM((2, 256, 512), BF16),
            pltpu.VMEM((8, 128), F32),
            pltpu.VMEM((16, 8, 128), F32),
            pltpu.VMEM((2, 8, 128), F32),
            pltpu.VMEM((4, 8, 128), F32),
            pltpu.VMEM((4, 8, 128), F32),
            pltpu.VMEM((4, 4, 256, 512), BF16),
            pltpu.VMEM((256, 512), F32),
            pltpu.VMEM((2, 2, 4, 64, 512), BF16),
            pltpu.VMEM((2, 2, 4, 64, 512), BF16),
            pltpu.VMEM((2, 2, 4, 64, 512), BF16),
            pltpu.VMEM((2, 2, 64, 512), BF16),
            pltpu.VMEM((2, 2, 64, 512), BF16),
            pltpu.VMEM((2, 2, 64, 512), BF16),
            dma((2, 2)), dma((2, 2, 8)), dma((2, 2, 8)), dma((16,)), dma((16,)),
            dma((2, 8)), dma((2, 8)), dma, dma((2,)), dma((2,)), dma((16,)), dma((16,)), dma((2,)),
            dma((2, 4)), dma((2, 4)), dma((3, 2, 2, 4)), dma((3, 2, 2, 4)), dma((3, 2, 2)), dma((3, 2, 2)),
        ],
        compiler_params=pltpu.CompilerParams(
            collective_id=0, has_side_effects=True, vmem_limit_bytes=30 << 20),
    )(*[pltpu.with_memory_space_constraint(a, pltpu.HBM) for a in (
        exit_layers.T, exit_scale, hidden_states, unembedding.reshape(32, 256, 256),
        targets.reshape(2, 128), norm_gain.reshape(64, 128))])
    return (grad, loss.reshape(()))


def solution(mesh):
    in_specs = (P(None, "dp", "vocab"), P("dp", None), P("dp"), P(), P(), P(None, "vocab"))
    out_specs = (P("dp", "vocab"), P())
    return jax.shard_map(
        per_device, mesh=mesh, in_specs=in_specs, out_specs=out_specs, check_vma=False
    )
```
